32 devices in a mesh: segment: 2 (over core), expert: 16 (over z, y, x).
Axes of the slice: x: 2, y: 2, z: 4, core: 2. Of those that a mesh axis runs over, the one named last changes fastest.
Arguments:
- fwd_tokens: bfloat16 [2, 1024, 2048], P('segment', 'expert'), may hold values from -6 to 6
- fwd_routes: int32 [2, 1024, 8], P('segment', 'expert'), may hold values from 0 to 15, all different within a row; in each aligned block of 64 rows (0 to 63, 64 to 127, ..., all dimensions but the last counted through in order) at most 48 rows name the same one
- fwd_gates: bfloat16 [2, 1024, 8], P('segment', 'expert'), may hold values from 0.049804688 to 0.5
- bwd_tokens: bfloat16 [2, 1024, 2048], P('segment', 'expert'), may hold values from -6 to 6
- bwd_routes: int32 [2, 1024, 8], P('segment', 'expert'), may hold values from 0 to 15, all different within a row; in each aligned block of 64 rows (0 to 63, 64 to 127, ..., all dimensions but the last counted through in order) at most 48 rows name the same one
- bwd_gates: bfloat16 [2, 1024, 8], P('segment', 'expert'), may hold values from 0.049804688 to 0.5
- cotangent: bfloat16 [2, 1024, 2048], P('segment', 'expert'), may hold values from -6 to 6
- w_gate_up: bfloat16 [2, 16, 2048, 1536], P('segment', 'expert'), may hold values from -0.125 to 0.125
- w_down: bfloat16 [2, 16, 768, 2048], P('segment', 'expert'), may hold values from -0.21875 to 0.21875
Outputs:
- forward_out: bfloat16 [2, 1024, 2048], P('segment', 'expert')
- input_grad: bfloat16 [2, 1024, 2048], P('segment', 'expert')
- gate_grad: bfloat16 [2, 1024, 8], P('segment', 'expert')
- grad_gate_up: bfloat16 [2, 16, 2048, 1536], P('segment', 'expert')
- grad_down: bfloat16 [2, 16, 768, 2048], P('segment', 'expert')
The draws below stay inside these ranges and needn't reach their ends.
Inputs may be any that keep to these rules, and one draw needn't show every extreme that they name: `fwd_routes`: each token names 8 different experts; within each aligned block of 64 tokens of one section no expert is named more than 48 times, a bound that some block reaches. `bwd_routes`: each token names 8 different experts; within each aligned block of 64 tokens of one section no expert is named more than 48 times, a bound that some block reaches.
All inputs are finite; a program needn't handle non-finite values.
Results may differ from the reference program's by a relative error of at most 0.015.
Values may be sent and summed in bfloat16 or wider, within the bound.
No kernel may reach another device: no remote copies, remote signals or barrier semaphores. Data moves between devices by JAX's collectives and lax.ppermute only.
A program may use at most 128 MiB of HBM per device.

```python
import math
import jax
import jax.numpy as jnp
import numpy as np
from jax import lax

D = 2048
FF = 768
TOP = 8
SECTIONS = 2
TOK_DEV = 64
EXPERTS = 16
TOKENS = 1024
CAP = 48
N_EXPERT = 16


def block_scale(own_key, shape, shards, least, high):
    level = 1.0
    for position, blocks in shards:
        heights = jax.random.uniform(jax.random.fold_in(jax.random.fold_in(own_key, 6), position), (blocks,), jnp.float32, least / len(shards), high / len(shards))
        level = level * jnp.repeat(jnp.exp(heights), shape[position] // blocks).reshape((-1,) + (1,) * (len(shape) - 1 - position))
    return level


def deal_out(stream_key, own, number, rows, number_of, top, reach, lean):
    sequence = jax.random.permutation(stream_key, number_of)
    crowded, usual = shares(number_of, rows * top, reach, lean, True), shares(number_of, rows * top, reach, lean, False)
    places = jnp.arange(number_of)

    def named(tallies, rotation):
        used = int((tallies > 0).sum())
        fixed = max(1, used // 4)
        passed = fixed + (places - fixed + rotation * (used - fixed)) % max(1, number_of - fixed)
        return jnp.zeros((number_of,), jnp.int32).at[sequence[jnp.where(places < fixed, places, passed)]].set(jnp.asarray(tallies, jnp.int32))

    tallies = jnp.where(number % 4 == 0, named(crowded, number // 4), named(usual, number - number // 4 - 1))
    mixed = jax.random.permutation(jax.random.fold_in(own, 3), number_of)
    giver, receiver = mixed[0:number_of // 2 * 2:2], mixed[1:number_of // 2 * 2:2]
    slack = jnp.minimum(tallies[giver] - 1, reach - tallies[receiver]) // 2
    slack = jnp.where((giver == sequence[0]) | (receiver == sequence[0]) | (tallies[receiver] == 0), 0, jnp.maximum(slack, 0))
    passed = jax.random.randint(jax.random.fold_in(own, 4), (number_of // 2,), 0, 1 << 20) % (slack + 1)
    tallies = tallies.at[giver].add(-passed).at[receiver].add(passed)
    items = jnp.searchsorted(jnp.cumsum(tallies), jnp.arange(rows * top), side="right").astype(jnp.int32)
    listing = items.reshape(top, rows).T
    listing = listing[jax.random.permutation(jax.random.fold_in(own, 1), rows)]
    rotation = jax.random.randint(jax.random.fold_in(own, 2), (rows, 1), 0, top)
    return jnp.take_along_axis(listing, (jnp.arange(top)[None, :] + rotation) % top, axis=1)


def shares(amount, total, limit, lean, full):
    loads = [(1 << 20) // math.isqrt(standing ** lean) + 1 for standing in range(1, amount + 1)]
    largest = limit if full else min(limit, max(-(-total // amount), total * loads[0] // sum(loads)))
    least = 1 if total - largest >= amount - 1 else 0
    counts, rest = [largest] + [least] * (amount - 1), total - largest - least * (amount - 1)
    while rest > 0:
        candidates = [i for i in range(1, amount) if counts[i] < largest] or [i for i in range(1, amount) if counts[i] < limit]
        whole, left = sum([loads[i] for i in candidates]), rest
        for i in candidates:
            extra = min(limit - counts[i], max(1, left * loads[i] // whole), rest)
            counts[i] = counts[i] + extra
            rest = rest - extra
    return np.array(counts)


def bell_draw(own_key, shape, scale, reach, cuts=(), held_as=jnp.bfloat16):
    array = jax.random.normal(own_key, shape, jnp.float32) * scale
    if len(cuts) > 0:
        array = block_scale(own_key, shape, cuts, -0.22, 0.18) * array
    return jnp.clip(array, min=-reach, max=reach).astype(held_as)


def setup_inputs(seed: int = 0) -> dict:
    arg_keys = jax.random.split(jax.random.key(seed), 10)
    fwd_tokens = bell_draw(arg_keys[0], (SECTIONS, TOKENS, D), 1.0, 6.0, ((0, 2), (1, 16)))
    fwd_routes_keys = jax.random.split(jax.random.fold_in(arg_keys[1], 1), SECTIONS * TOKENS // TOK_DEV)
    fwd_routes_turns = jax.random.permutation(jax.random.fold_in(arg_keys[1], 3), SECTIONS * TOKENS // TOK_DEV)
    fwd_routes = jax.vmap(lambda own, number: deal_out(jax.random.fold_in(arg_keys[1], 2), own, number, TOK_DEV, EXPERTS, TOP, CAP, 2))(fwd_routes_keys, fwd_routes_turns).reshape((SECTIONS, TOKENS, TOP))
    fwd_gates = jnp.clip(jnp.exp(math.log(0.5) - 2.306499 * jax.random.uniform(arg_keys[2], (SECTIONS, TOKENS, TOP), jnp.float32) ** block_scale(arg_keys[2], (SECTIONS, TOKENS, TOP), ((0, 2), (1, 16)), -0.2, 0.2)), 0.049804688, 0.5).astype(jnp.bfloat16)
    bwd_tokens = bell_draw(arg_keys[3], (SECTIONS, TOKENS, D), 1.0, 6.0, ((0, 2), (1, 16)))
    bwd_routes_keys = jax.random.split(jax.random.fold_in(arg_keys[4], 1), SECTIONS * TOKENS // TOK_DEV)
    bwd_routes_turns = jax.random.permutation(jax.random.fold_in(arg_keys[4], 3), SECTIONS * TOKENS // TOK_DEV)
    bwd_routes = jax.vmap(lambda own, number: deal_out(jax.random.fold_in(arg_keys[4], 2), own, number, TOK_DEV, EXPERTS, TOP, CAP, 2))(bwd_routes_keys, bwd_routes_turns).reshape((SECTIONS, TOKENS, TOP))
    bwd_gates = jnp.clip(jnp.exp(math.log(0.5) - 2.306499 * jax.random.uniform(arg_keys[5], (SECTIONS, TOKENS, TOP), jnp.float32) ** block_scale(arg_keys[5], (SECTIONS, TOKENS, TOP), ((0, 2), (1, 16)), -0.2, 0.2)), 0.049804688, 0.5).astype(jnp.bfloat16)
    cotangent = bell_draw(arg_keys[6], (SECTIONS, TOKENS, D), 1.0, 6.0, ((0, 2), (1, 16)))
    w_gate_up = bell_draw(arg_keys[7], (SECTIONS, EXPERTS, D, 2 * FF), D ** -0.5, 0.125, ((0, 2), (1, 16)))
    w_down = bell_draw(arg_keys[8], (SECTIONS, EXPERTS, FF, D), FF ** -0.5, 0.21875, ((0, 2), (1, 16)))
    return dict(fwd_tokens=fwd_tokens, fwd_routes=fwd_routes, fwd_gates=fwd_gates, bwd_tokens=bwd_tokens, bwd_routes=bwd_routes, bwd_gates=bwd_gates, cotangent=cotangent, w_gate_up=w_gate_up, w_down=w_down)


def slot_index(routes):
    blocks = routes.reshape(N_EXPERT, TOK_DEV * TOP)
    onehot = (blocks[:, :, None] == jnp.arange(EXPERTS, dtype=jnp.int32)[None, None, :]).astype(jnp.int32)
    rank = jnp.sum((jnp.cumsum(onehot, axis=1) - onehot) * onehot, axis=-1)
    source = jnp.arange(N_EXPERT, dtype=jnp.int32)[:, None]
    slot = blocks * (N_EXPERT * CAP) + source * CAP + rank
    return slot.reshape(-1).astype(jnp.int32)


def fill_rows(values, slot, width):
    rows = jnp.repeat(values, TOP, axis=0)
    buffer = jnp.zeros((EXPERTS * N_EXPERT * CAP, width), values.dtype)
    return buffer.at[slot].set(rows)


def expert_forward(rows, w_gu, w_dn):
    hidden = jnp.dot(rows, w_gu, preferred_element_type=jnp.float32)
    gate = hidden[:, :FF]
    upper = hidden[:, FF:]
    active = (gate * jax.nn.sigmoid(gate) * upper).astype(jnp.bfloat16)
    return jnp.dot(active, w_dn, preferred_element_type=jnp.float32).astype(jnp.bfloat16)


def expert_backward(rows, grads, gates, w_gu, w_dn):
    hidden = jnp.dot(rows, w_gu, preferred_element_type=jnp.float32)
    gate = hidden[:, :FF]
    upper = hidden[:, FF:]
    sigma = jax.nn.sigmoid(gate)
    silu_part = gate * sigma
    active = (silu_part * upper).astype(jnp.bfloat16)
    output = jnp.dot(active, w_dn, preferred_element_type=jnp.float32).astype(jnp.bfloat16)
    slot_gg = jnp.sum(output.astype(jnp.float32) * grads.astype(jnp.float32), axis=-1).astype(jnp.bfloat16)
    scaled = (gates.astype(jnp.float32)[:, None] * grads.astype(jnp.float32)).astype(jnp.bfloat16)
    grad_dn = lax.dot_general(active, scaled, (((0,), (0,)), ((), ())), preferred_element_type=jnp.float32).astype(jnp.bfloat16)
    d_active = lax.dot_general(scaled, w_dn, (((1,), (1,)), ((), ())), preferred_element_type=jnp.float32)
    d_gate = d_active * upper * sigma * (1.0 + gate * (1.0 - sigma))
    d_upper = d_active * silu_part
    d_hidden = jnp.concatenate([d_gate, d_upper], axis=-1).astype(jnp.bfloat16)
    grad_gu = lax.dot_general(rows, d_hidden, (((0,), (0,)), ((), ())), preferred_element_type=jnp.float32).astype(jnp.bfloat16)
    d_rows = lax.dot_general(d_hidden, w_gu, (((1,), (1,)), ((), ())), preferred_element_type=jnp.float32).astype(jnp.bfloat16)
    return d_rows, slot_gg, grad_gu, grad_dn


def reference(fwd_tokens, fwd_routes, fwd_gates, bwd_tokens, bwd_routes, bwd_gates, cotangent, w_gate_up, w_down):
    rows_exp = N_EXPERT * CAP
    combined_all = []
    token_all = []
    gg_all = []
    ggu_all = []
    gdn_all = []
    for section in range(SECTIONS):
        slot = slot_index(fwd_routes[section])
        buffer = fill_rows(fwd_tokens[section], slot, D).reshape(EXPERTS, rows_exp, D)
        outputs = lax.map(lambda item: expert_forward(item[0], item[1], item[2]), (buffer, w_gate_up[section], w_down[section]))
        picked = outputs.reshape(-1, D)[slot].reshape(TOKENS, TOP, D).astype(jnp.float32)
        weights = fwd_gates[section].astype(jnp.float32)
        combined_all.append(jnp.sum(weights[:, :, None] * picked, axis=1).astype(jnp.bfloat16))

        slot_b = slot_index(bwd_routes[section])
        rows_b = fill_rows(bwd_tokens[section], slot_b, D).reshape(EXPERTS, rows_exp, D)
        grads_b = fill_rows(cotangent[section], slot_b, D).reshape(EXPERTS, rows_exp, D)
        gates_b = jnp.zeros((EXPERTS * rows_exp,), jnp.bfloat16).at[slot_b].set(bwd_gates[section].reshape(-1)).reshape(EXPERTS, rows_exp)
        d_rows, slot_gg, grad_gu, grad_dn = lax.map(
            lambda item: expert_backward(item[0], item[1], item[2], item[3], item[4]),
            (rows_b, grads_b, gates_b, w_gate_up[section], w_down[section]))
        picked_d = d_rows.reshape(-1, D)[slot_b].reshape(TOKENS, TOP, D).astype(jnp.float32)
        token_all.append(jnp.sum(picked_d, axis=1).astype(jnp.bfloat16))
        gg_all.append(slot_gg.reshape(-1)[slot_b].reshape(TOKENS, TOP))
        ggu_all.append(grad_gu)
        gdn_all.append(grad_dn)
    forward_out = jnp.stack([combined_all[1], combined_all[0]])
    input_grad = jnp.stack([token_all[1], token_all[0]])
    gate_grad = jnp.stack([gg_all[1], gg_all[0]])
    return forward_out, input_grad, gate_grad, jnp.stack(ggu_all), jnp.stack(gdn_all)
```

```python
import jax
import jax.numpy as jnp
from jax import lax
from jax.experimental import pallas as pl
from jax.experimental.pallas import tpu as pltpu
from jax.sharding import PartitionSpec as P

LANES = 128
F32 = jnp.float32
BF16 = jnp.bfloat16
NT = (((1,), (1,)), ((), ()))
TN = (((0,), (0,)), ((), ()))
VMEM_BYTES = 50 << 20


def send(array, size, bit):
    return lax.ppermute(array, "expert", [(i, i ^ (1 << bit)) for i in range(size)])


def after(array, *others):
    return lax.optimization_barrier((array, *others))[0]


def spread(rows, size, late):
    bits = size.bit_length() - 1
    count, width = rows.shape
    half = count // 2
    top = jnp.stack([rows, send(rows, size, bits - 1)])
    if late:
        block = top[:, :half], top[:, half:]
        block = jnp.stack([jnp.stack([p, send(p, size, b)]) for b, p in enumerate(block)])
        block = block[:, None]
        for bit in range(2, bits - 1):
            block = jnp.concatenate([block, send(block, size, bit)], axis=1)
        block = block[0], block[1]
    else:
        block = top[None]
        for bit in range(2, bits - 1):
            block = jnp.concatenate([block, send(block, size, bit)])
        block = block[:, :, :half], block[:, :, half:]
        block = [jnp.stack([p, send(p, size, b)], axis=1) for b, p in enumerate(block)]
    kept = [p.reshape(-1, width) for p in block]
    arrived = [send(p, size, 1 - b) for b, p in enumerate(kept)]
    return kept, arrived


def add(a, b):
    return (a.astype(F32) + b.astype(F32)).astype(BF16)


def collect(kept, away, size, late):
    bits = size.bit_length() - 1
    width = kept[0].shape[1]
    middle = 1 << (bits - 3)
    got = [send(p, size, 1 - b) for b, p in enumerate(away)]
    shape = (middle, 2, 2, -1, width)
    part = [add(k, g).reshape(shape) for k, g in zip(kept, got)]
    if late:
        part = jnp.stack(part)
        for bit in range(bits - 2, 1, -1):
            n = part.shape[1] // 2
            part = add(part[:, :n], send(part[:, n:], size, bit))
        part = [part[b, 0] for b in range(2)]
        part = jnp.concatenate([add(p[0], send(p[1], size, b)) for b, p in enumerate(part)], axis=1)
    else:
        part = jnp.concatenate([add(p[:, 0], send(p[:, 1], size, b)) for b, p in enumerate(part)], axis=2)
        for bit in range(bits - 2, 1, -1):
            n = part.shape[0] // 2
            part = add(part[:n], send(part[n:], size, bit))
        part = part[0]
    sections = lax.axis_size("segment")
    cross = lambda flip: [
        (s * size + i, (s ^ 1) * size + (i ^ flip)) for s in range(sections) for i in range(size)
    ]
    own = lax.ppermute(part[0], ("segment", "expert"), cross(0))
    other = lax.ppermute(part[1], ("segment", "expert"), cross(1 << (bits - 1)))
    return own.astype(F32) + other.astype(F32)


def dense_gates(routes, gates, size):
    hit = routes[:, :, None] == jnp.arange(size, dtype=jnp.int32)[None, None, :]
    return jnp.sum(jnp.where(hit, gates[:, :, None].astype(F32), 0.0), axis=1)


def pick(table, at):
    lane = lax.broadcasted_iota(jnp.int32, table.shape, 1)
    return jnp.sum(jnp.where(lane == at, table.astype(F32), 0.0), axis=1, keepdims=True)


def back_kernel(me_ref, x_ref, dy_ref, wgu_ref, wdn_ref, dx_ref, dh_ref, wa_ref):
    me = me_ref[0]
    ff, width = wdn_ref.shape
    gate_b = pick(x_ref[:, width:], me)
    hidden = jnp.dot(x_ref[:, :width], wgu_ref[...], preferred_element_type=F32)
    gate = hidden[:, :ff]
    upper = hidden[:, ff:]
    back = lax.dot_general(dy_ref[...], wdn_ref[...], NT, preferred_element_type=F32)
    sigma = jax.nn.sigmoid(gate)
    silu = gate * sigma
    active = silu * upper
    gate_grad = jnp.sum(active * back, axis=1, keepdims=True)
    wa_ref[...] = (active * gate_b).astype(BF16)
    d_active = back * gate_b
    dh_ref[:, :ff] = (d_active * upper * sigma * (1.0 + gate * (1.0 - sigma))).astype(BF16)
    dh_ref[:, ff:] = (d_active * silu).astype(BF16)
    dx_ref[:, :width] = lax.dot_general(
        dh_ref[...], wgu_ref[...], NT, preferred_element_type=F32
    ).astype(BF16)
    lane = lax.broadcasted_iota(jnp.int32, (x_ref.shape[0], dx_ref.shape[1] - width), 1)
    dx_ref[:, width:] = jnp.where(lane == me, gate_grad, 0.0).astype(BF16)


def row_tile(rows):
    return min(rows, 256)


def back_rows(me, x, dy, w_gu, w_dn):
    rows, wide = x.shape
    ff, width = w_dn.shape
    tile = row_tile(rows)
    row = lambda w: pl.BlockSpec((tile, w), lambda i, m: (i, 0))
    full = lambda a: pl.BlockSpec(a.shape, lambda i, m: (0, 0), pipeline_mode=pl.Buffered(1))
    out = lambda w: jax.ShapeDtypeStruct((rows, w), BF16)
    return pl.pallas_call(
        back_kernel,
        grid_spec=pltpu.PrefetchScalarGridSpec(
            num_scalar_prefetch=1,
            grid=(rows // tile,),
            in_specs=[row(wide), row(width), full(w_gu), full(w_dn)],
            out_specs=[row(wide), row(2 * ff), row(ff)],
        ),
        out_shape=[out(wide), out(2 * ff), out(ff)],
        compiler_params=pltpu.CompilerParams(vmem_limit_bytes=VMEM_BYTES),
        cost_estimate=pl.CostEstimate(
            flops=rows * width * ff * 10,
            bytes_accessed=6 * ff * width + rows * (4 * wide + 2 * width + 6 * ff),
            transcendentals=rows * ff,
        ),
    )(me, x, dy, w_gu, w_dn)


def forward_kernel(me_ref, x_ref, table_ref, wgu_ref, wdn_ref, y_ref):
    ff, width = wdn_ref.shape
    gate_f = pick(table_ref[...], me_ref[1])
    hidden = jnp.dot(x_ref[...], wgu_ref[...], preferred_element_type=F32)
    gate = hidden[:, :ff]
    active = (gate * jax.nn.sigmoid(gate) * hidden[:, ff:]).astype(BF16)
    y_ref[...] = (jnp.dot(active, wdn_ref[...], preferred_element_type=F32) * gate_f).astype(BF16)


def forward_rows(me, x, table, w_gu, w_dn):
    rows = x.shape[0]
    ff, width = w_dn.shape
    lanes = table.shape[1] - width
    tile = row_tile(rows)
    row = pl.BlockSpec((tile, width), lambda i, m: (i, 0))
    full = lambda a: pl.BlockSpec(a.shape, lambda i, m: (0, 0), pipeline_mode=pl.Buffered(1))
    return pl.pallas_call(
        forward_kernel,
        grid_spec=pltpu.PrefetchScalarGridSpec(
            num_scalar_prefetch=1,
            grid=(rows // tile,),
            in_specs=[
                row,
                pl.BlockSpec((tile, lanes), lambda i, m: (i, width // lanes)),
                full(w_gu),
                full(w_dn),
            ],
            out_specs=row,
        ),
        out_shape=jax.ShapeDtypeStruct((rows, width), BF16),
        compiler_params=pltpu.CompilerParams(vmem_limit_bytes=VMEM_BYTES),
        cost_estimate=pl.CostEstimate(
            flops=rows * width * ff * 6,
            bytes_accessed=6 * ff * width + rows * 4 * width,
            transcendentals=rows * ff,
        ),
    )(me, x, table, w_gu, w_dn)


def weight_kernel(*refs):
    count = (len(refs) - 2) // 2
    out_ref, total = refs[-2:]
    step = pl.program_id(1)

    @pl.when(step == 0)
    def _():
        total[...] = jnp.zeros_like(total)

    for left, right in zip(refs[:count], refs[count : 2 * count]):
        total[...] += lax.dot_general(left[...], right[...], TN, preferred_element_type=F32)

    @pl.when(step == pl.num_programs(1) - 1)
    def _():
        out_ref[...] = total[...].astype(BF16)


def weight_grad(left, right, rows_out, tile_out):
    rows = left[0].shape[0]
    tile = row_tile(rows)
    cols = right[0].shape[1]
    return pl.pallas_call(
        weight_kernel,
        grid=(rows_out // tile_out, rows // tile),
        in_specs=[pl.BlockSpec((tile, tile_out), lambda i, j: (j, i)) for _ in left]
        + [pl.BlockSpec((tile, cols), lambda i, j: (j, 0)) for _ in right],
        out_specs=pl.BlockSpec((tile_out, cols), lambda i, j: (i, 0)),
        out_shape=jax.ShapeDtypeStruct((rows_out, cols), BF16),
        scratch_shapes=[pltpu.VMEM((tile_out, cols), F32)],
        compiler_params=pltpu.CompilerParams(vmem_limit_bytes=VMEM_BYTES),
        cost_estimate=pl.CostEstimate(
            flops=2 * len(left) * rows * rows_out * cols,
            bytes_accessed=2 * len(left) * rows * (rows_out + cols) + 2 * rows_out * cols,
            transcendentals=0,
        ),
    )(*left, *right)


def shards(
    fwd_tokens,
    fwd_routes,
    fwd_gates,
    bwd_tokens,
    bwd_routes,
    bwd_gates,
    cotangent,
    w_gate_up,
    w_down,
):
    size = lax.axis_size("expert")
    me = lax.axis_index("expert")
    width = fwd_tokens.shape[2]
    w_gu = w_gate_up[0, 0]
    w_dn = w_down[0, 0]
    ff = w_dn.shape[0]
    sections = lax.axis_size("segment")
    swap = [(s, s ^ 1) for s in range(sections)]
    other_routes = lax.ppermute(bwd_routes[0], "segment", swap)
    table = jnp.concatenate(
        [
            dense_gates(bwd_routes[0], bwd_gates[0], size),
            dense_gates(fwd_routes[0], fwd_gates[0], size),
        ],
        axis=1,
    )
    table = jnp.pad(table, ((0, 0), (0, -table.shape[1] % LANES))).astype(BF16)
    places = jnp.stack([me, me + size]).astype(jnp.int32)

    x_in = jnp.concatenate([bwd_tokens[0], table], axis=1)
    x_kept, x_new = spread(x_in, size, False)
    dy_kept, dy_new = spread(cotangent[0], size, True)
    xf_kept, xf_new = spread(fwd_tokens[0], size, True)

    def back(xs, dys):
        return zip(*[back_rows(places, x, dy, w_gu, w_dn) for x, dy in zip(xs, dys)])

    dx_kept, dh_kept, wa_kept = back(x_kept, dy_kept)
    dx_new, dh_new, wa_new = back(x_new, dy_new)
    home = collect(dx_kept, dx_new, size, True)

    y_new = [forward_rows(places, x, t, w_gu, w_dn) for x, t in zip(xf_new, x_new)]
    y_kept = [forward_rows(places, x, t, w_gu, w_dn) for x, t in zip(xf_kept, x_kept)]
    combined = collect(y_kept, y_new, size, False).astype(BF16)

    grad_gu = weight_grad([*x_kept, *x_new], [*dh_kept, *dh_new], width, width // 4)
    grad_dn = weight_grad([*wa_kept, *wa_new], [*dy_kept, *dy_new], ff, ff // 3)

    token_grad = home[:, :width].astype(BF16)
    hit = other_routes[:, :, None] == jnp.arange(size, dtype=jnp.int32)[None, None, :]
    gate_home = jnp.sum(jnp.where(hit, home[:, None, width : width + size], 0.0), axis=2)
    return (
        combined[None],
        token_grad[None],
        gate_home.astype(BF16)[None],
        grad_gu[None, None],
        grad_dn[None, None],
    )


def solution(mesh):
    three = P("segment", "expert", None)
    four = P("segment", "expert", None, None)
    return jax.shard_map(
        shards,
        mesh=mesh,
        in_specs=(three,) * 7 + (four,) * 2,
        out_specs=(three,) * 3 + (four,) * 2,
        check_vma=False,
    )
```

```python
import jax
import jax.numpy as jnp
from jax import lax
from jax.experimental import pallas as pl
from jax.experimental.pallas import tpu as pltpu
from jax.sharding import PartitionSpec as P


LANES = 128
F32 = jnp.float32
BF16 = jnp.bfloat16
NT = (((1,), (1,)), ((), ()))
TN = (((0,), (0,)), ((), ()))
VMEM_BYTES = 50 << 20
ANY = pl.BlockSpec(memory_space=pl.ANY)


def after(value, *others):
    return lax.optimization_barrier((value, *others))[0]


def send(array, size, bit):
    return lax.ppermute(array, "expert", [(i, i ^ (1 << bit)) for i in range(size)])


def three_ways(size, count):
    bits = size.bit_length() - 1
    middle = list(range(2, bits - 1))
    small, large = count // 4, 3 * count // 8
    return [
        (0, small, [0, 1, *middle]),
        (small, small + large, [1, *middle, 0]),
        (small + large, count, [*middle, 0, 1]),
    ]


def send_all(arrays, size, parts, step):
    bits = [p[2][step] for p in parts]
    got = [None] * len(arrays)
    for bit in dict.fromkeys(bits):
        which = [i for i, b in enumerate(bits) if b == bit]
        whole = send(jnp.concatenate([arrays[i] for i in which]), size, bit)
        start = 0
        for i in which:
            got[i] = whole[start : start + arrays[i].shape[0]]
            start += arrays[i].shape[0]
    return got


def top_bit(size):
    return size.bit_length() - 2


def spread_rest(kept, size, parts):
    for step in range(len(parts[0][2]) - 1):
        got = send_all(kept, size, parts, step)
        kept = [jnp.concatenate([k, g]) for k, g in zip(kept, got)]
    return kept, send_all(kept, size, parts, -1)


def add(a, b):
    return (a.astype(F32) + b.astype(F32)).astype(BF16)


def collect_first(kept, away, size, parts, hold):
    got = after(send_all(away, size, parts, -1), *hold)
    return [add(k, g) for k, g in zip(kept, got)]


def collect_rest(rows, size, parts):
    for step in range(len(parts[0][2]) - 2, -1, -1):
        half = [r.shape[0] // 2 for r in rows]
        got = send_all([r[n:] for r, n in zip(rows, half)], size, parts, step)
        rows = [add(r[:n], g) for r, n, g in zip(rows, half, got)]
    sections = lax.axis_size("segment")
    cross = lambda flip: [
        (s * size + i, (s ^ 1) * size + (i ^ flip)) for s in range(sections) for i in range(size)
    ]
    own = jnp.concatenate([r[: r.shape[0] // 2] for r in rows])
    other = jnp.concatenate([r[r.shape[0] // 2 :] for r in rows])
    other = lax.ppermute(other, ("segment", "expert"), cross(size // 2))
    own = lax.ppermute(own, ("segment", "expert"), cross(0))
    return own.astype(F32) + other.astype(F32)


def dense_gates(routes, gates, size):
    hit = routes[:, :, None] == jnp.arange(size, dtype=jnp.int32)[None, None, :]
    return jnp.sum(jnp.where(hit, gates[:, :, None].astype(F32), 0.0), axis=1)


def pick(table, at):
    lane = lax.broadcasted_iota(jnp.int32, table.shape, 1)
    return jnp.sum(jnp.where(lane == at, table.astype(F32), 0.0), axis=1, keepdims=True)


class Copies:
    def __init__(self, sems):
        self.sems = sems
        self.used = 0

    def make(self, source, target):
        copy = pltpu.make_async_copy(source, target, self.sems.at[self.used])
        self.used += 1
        return copy


def starts_of(counts):
    return [sum(counts[:i]) for i in range(len(counts))]


def block_start(step, count):
    return step * count if isinstance(step, int) else pl.multiple_of(step * count, 8)


def row_copies(copies, pieces, whole, counts, step, columns, outward=False):
    made = []
    for piece, count, start in zip(pieces, counts, starts_of(counts)):
        outer = piece.at[pl.ds(block_start(step, count), count), columns]
        inner = whole.at[pl.ds(start, count)]
        made.append(copies.make(inner, outer) if outward else copies.make(outer, inner))
    return made


def begin(made):
    for copy in made:
        copy.start()


def end(made):
    for copy in made:
        copy.wait()


def once(groups, step):
    return pl.when(step == 0) if groups > 1 else lambda run: run()


def load_weights(copies, groups, step, wgu_ref, wdn_ref, wgu, wdn, chunks):
    ff = wdn.shape[0]
    wide = ff // chunks
    per_chunk = []
    for j in range(chunks):
        made = []
        for at in (j * wide, ff + j * wide):
            made.append(copies.make(wgu_ref.at[:, pl.ds(at, wide)], wgu.at[:, pl.ds(at, wide)]))
        made.append(copies.make(wdn_ref.at[pl.ds(j * wide, wide)], wdn.at[pl.ds(j * wide, wide)]))
        per_chunk.append(made)

    def start(j):
        @once(groups, step)
        def _():
            begin(per_chunk[j])

    def ready(j):
        @once(groups, step)
        def _():
            end(per_chunk[j])

    return start, ready


CHUNKS = 3
PANELS = 4
SPANS = 2


def back_kernel(counts, groups, me_ref, *refs):
    n = len(counts)
    xd_in, (wgu_ref, wdn_ref) = refs[:n], refs[n : n + 2]
    dx_out, (dh_out, wa_out) = refs[n + 2 : 2 * n + 2], refs[2 * n + 2 : 2 * n + 4]
    x, dy, table, wgu, wdn, dx, extra, dh, wa, sems = refs[2 * n + 4 :]
    me = me_ref[0]
    step = pl.program_id(0) if groups > 1 else 0
    ff, width = wdn.shape
    lanes = table.shape[1]
    rows = x.shape[0]
    copies = Copies(sems)
    ins = row_copies(copies, xd_in, x, counts, step, pl.ds(0, width))
    dys = row_copies(copies, xd_in, dy, counts, step, pl.ds(width, width))
    dys += row_copies(copies, xd_in, table, counts, step, pl.ds(2 * width, lanes))
    here = pl.ds(block_start(step, rows), rows)
    begin(ins)
    start, ready = load_weights(copies, groups, step, wgu_ref, wdn_ref, wgu, wdn, CHUNKS)
    start(0)
    begin(dys)
    for j in range(1, CHUNKS):
        start(j)
    end(ins)
    wide = ff // CHUNKS
    gate_grad = jnp.zeros((rows, 1), F32)
    for j in range(CHUNKS):
        ready(j)
        own = pl.ds(j * wide, wide)
        also = pl.ds(ff + j * wide, wide)
        gate = jnp.dot(x[...], wgu[:, own], preferred_element_type=F32)
        upper = jnp.dot(x[...], wgu[:, also], preferred_element_type=F32)
        if j == 0:
            end(dys)
            gate_b = pick(table[...], me)
        back = lax.dot_general(dy[...], wdn[own], NT, preferred_element_type=F32)
        sigma = jax.nn.sigmoid(gate)
        silu = gate * sigma
        active = silu * upper
        gate_grad += jnp.sum(active * back, axis=1, keepdims=True)
        wa[:, own] = (active * gate_b).astype(BF16)
        d_active = back * gate_b
        dh[:, own] = (d_active * upper * sigma * (1.0 + gate * (1.0 - sigma))).astype(BF16)
        dh[:, also] = (d_active * silu).astype(BF16)
    lane = lax.broadcasted_iota(jnp.int32, (rows, lanes), 1)
    extra[...] = jnp.where(lane == me, gate_grad, 0.0).astype(BF16)
    outs = row_copies(copies, dx_out, extra, counts, step, pl.ds(width, lanes), True)
    outs += [copies.make(dh, dh_out.at[here]), copies.make(wa, wa_out.at[here])]
    begin(outs)
    panel = width // PANELS
    for p in range(PANELS):
        dx[p] = lax.dot_general(
            dh[...], wgu[pl.ds(p * panel, panel)], NT, preferred_element_type=F32
        ).astype(BF16)
        made = row_copies(copies, dx_out, dx.at[p], counts, step, pl.ds(p * panel, panel), True)
        begin(made)
        outs += made
    end(outs)


def group_counts(pieces, groups):
    return [p.shape[0] // groups for p in pieces]


def back_rows(me, xds, w_gu, w_dn, groups):
    ff, width = w_dn.shape
    lanes = xds[0].shape[1] - 2 * width
    counts = group_counts(xds, groups)
    rows = sum(counts)
    n = len(counts)
    total = rows * groups
    shape = jax.ShapeDtypeStruct
    out = pl.pallas_call(
        lambda *refs: back_kernel(counts, groups, *refs),
        grid_spec=pltpu.PrefetchScalarGridSpec(
            num_scalar_prefetch=1,
            grid=(groups,),
            in_specs=[ANY] * (n + 2),
            out_specs=[ANY] * (n + 2),
            scratch_shapes=[
                pltpu.VMEM((rows, width), BF16),
                pltpu.VMEM((rows, width), BF16),
                pltpu.VMEM((rows, lanes), BF16),
                pltpu.VMEM(w_gu.shape, BF16),
                pltpu.VMEM(w_dn.shape, BF16),
                pltpu.VMEM((PANELS, rows, width // PANELS), BF16),
                pltpu.VMEM((rows, lanes), BF16),
                pltpu.VMEM((rows, 2 * ff), BF16),
                pltpu.VMEM((rows, ff), BF16),
                pltpu.SemaphoreType.DMA((n * (4 + PANELS) + 3 * CHUNKS + 2,)),
            ],
        ),
        out_shape=[shape((p.shape[0], width + lanes), BF16) for p in xds]
        + [shape((total, 2 * ff), BF16), shape((total, ff), BF16)],
        compiler_params=pltpu.CompilerParams(vmem_limit_bytes=VMEM_BYTES),
        cost_estimate=pl.CostEstimate(
            flops=total * width * ff * 10,
            bytes_accessed=6 * ff * width + total * (6 * width + 4 * lanes + 6 * ff),
            transcendentals=total * ff,
        ),
    )(me, *xds, w_gu, w_dn)
    return out[:n], out[n], out[n + 1]


def forward_kernel(counts, groups, me_ref, *refs):
    n = len(counts)
    x_in, (wgu_ref, wdn_ref), y_out = refs[:n], refs[n : n + 2], refs[n + 2 : 2 * n + 2]
    x, table, wgu, wdn, act, y, sems = refs[2 * n + 2 :]
    step = pl.program_id(0) if groups > 1 else 0
    ff, width = wdn.shape
    lanes = table.shape[1]
    copies = Copies(sems)
    ins = row_copies(copies, x_in, x, counts, step, pl.ds(0, width))
    ins += row_copies(copies, x_in, table, counts, step, pl.ds(width, lanes))
    begin(ins)
    start, ready = load_weights(copies, groups, step, wgu_ref, wdn_ref, wgu, wdn, CHUNKS)
    for j in range(CHUNKS):
        start(j)
    end(ins)
    outs = []
    gate_f = pick(table[...], me_ref[1])
    wide = ff // CHUNKS
    for j in range(CHUNKS):
        ready(j)
        own = pl.ds(j * wide, wide)
        also = pl.ds(ff + j * wide, wide)
        gate = jnp.dot(x[...], wgu[:, own], preferred_element_type=F32)
        upper = jnp.dot(x[...], wgu[:, also], preferred_element_type=F32)
        act[:, own] = (gate * jax.nn.sigmoid(gate) * upper).astype(BF16)
    panel = width // PANELS
    for p in range(PANELS):
        cols = pl.ds(p * panel, panel)
        y[p] = (jnp.dot(act[...], wdn[:, cols], preferred_element_type=F32) * gate_f).astype(BF16)
        made = row_copies(copies, y_out, y.at[p], counts, step, cols, True)
        begin(made)
        outs += made
    end(outs)


def forward_rows(me, xs, w_gu, w_dn, groups):
    ff, width = w_dn.shape
    lanes = xs[0].shape[1] - width
    counts = group_counts(xs, groups)
    rows = sum(counts)
    n = len(counts)
    total = rows * groups
    return pl.pallas_call(
        lambda *refs: forward_kernel(counts, groups, *refs),
        grid_spec=pltpu.PrefetchScalarGridSpec(
            num_scalar_prefetch=1,
            grid=(groups,),
            in_specs=[ANY] * (n + 2),
            out_specs=[ANY] * n,
            scratch_shapes=[
                pltpu.VMEM((rows, width), BF16),
                pltpu.VMEM((rows, lanes), BF16),
                pltpu.VMEM(w_gu.shape, BF16),
                pltpu.VMEM(w_dn.shape, BF16),
                pltpu.VMEM((rows, ff), BF16),
                pltpu.VMEM((PANELS, rows, width // PANELS), BF16),
                pltpu.SemaphoreType.DMA((n * (2 + PANELS) + 3 * CHUNKS,)),
            ],
        ),
        out_shape=[jax.ShapeDtypeStruct((p.shape[0], width), BF16) for p in xs],
        compiler_params=pltpu.CompilerParams(vmem_limit_bytes=VMEM_BYTES),
        cost_estimate=pl.CostEstimate(
            flops=total * width * ff * 6,
            bytes_accessed=6 * ff * width + total * 4 * width,
            transcendentals=total * ff,
        ),
    )(me, *xs, w_gu, w_dn)


def weight_kernel(lefts, rights, left_at, right_at, groups, *refs):
    n, m = len(lefts), len(rights)
    left_in, right_in, out_ref = refs[:n], refs[n : n + m], refs[n + m]
    left, right, stage = refs[n + m + 1 : n + m + 4]
    sems = refs[-1]
    step = pl.program_id(0) if groups > 1 else 0
    copies = Copies(sems)
    tile = stage.shape[1]
    tiles = range(stage.shape[0])
    span = right.shape[0] // SPANS
    made = row_copies(copies, right_in, right, rights, step, pl.ds(right_at, right.shape[1]))
    begin(made)
    columns = [
        row_copies(copies, left_in, left.at[t], lefts, step, pl.ds(left_at + t * tile, tile))
        for t in tiles
    ]
    for t in tiles:
        begin(columns[t])
    end(made)
    outs = []
    for t in tiles:
        end(columns[t])
        part = sum(
            lax.dot_general(
                left[t, pl.ds(r, span)], right[pl.ds(r, span)], TN, preferred_element_type=F32
            )
            for r in range(0, right.shape[0], span)
        )
        if groups > 1:
            total = refs[n + m + 4]
            part += jnp.where(step == 0, 0.0, total[t])
            total[t] = part
        stage[t] = part.astype(BF16)
        outs.append(copies.make(stage.at[t], out_ref.at[pl.ds(t * tile, tile)]))
        if groups == 1:
            outs[-1].start()
    if groups == 1:
        end(outs)
    else:

        @pl.when(step == groups - 1)
        def _():
            begin(outs)
            end(outs)


def weight_grad(lefts, rights, left_at, left_wide, right_at, right_wide, groups):
    left_counts = group_counts(lefts, groups)
    right_counts = group_counts(rights, groups)
    rows = sum(left_counts)
    tile = 512 if left_wide % 512 == 0 else 256
    tiles = left_wide // tile
    scratch = [
        pltpu.VMEM((tiles, rows, tile), BF16),
        pltpu.VMEM((rows, right_wide), BF16),
        pltpu.VMEM((tiles, tile, right_wide), BF16),
    ]
    if groups > 1:
        scratch.append(pltpu.VMEM((tiles, tile, right_wide), F32))
    scratch.append(pltpu.SemaphoreType.DMA((tiles * len(lefts) + len(rights) + tiles,)))
    return pl.pallas_call(
        lambda *refs: weight_kernel(left_counts, right_counts, left_at, right_at, groups, *refs),
        grid=(groups,),
        in_specs=[ANY] * (len(lefts) + len(rights)),
        out_specs=ANY,
        out_shape=jax.ShapeDtypeStruct((left_wide, right_wide), BF16),
        scratch_shapes=scratch,
        compiler_params=pltpu.CompilerParams(vmem_limit_bytes=VMEM_BYTES),
        cost_estimate=pl.CostEstimate(
            flops=2 * rows * groups * left_wide * right_wide,
            bytes_accessed=2 * rows * groups * (left_wide + right_wide) + 2 * left_wide * right_wide,
            transcendentals=0,
        ),
    )(*lefts, *rights)


def shards(
    fwd_tokens,
    fwd_routes,
    fwd_gates,
    bwd_tokens,
    bwd_routes,
    bwd_gates,
    cotangent,
    w_gate_up,
    w_down,
):
    size = lax.axis_size("expert")
    me = lax.axis_index("expert")
    count, width = fwd_tokens.shape[1:]
    w_gu = w_gate_up[0, 0]
    w_dn = w_down[0, 0]
    ff = w_dn.shape[0]
    groups = max(1, size // 16)
    sections = lax.axis_size("segment")
    swap = [(s, s ^ 1) for s in range(sections)]
    table = jnp.concatenate(
        [
            dense_gates(bwd_routes[0], bwd_gates[0], size),
            dense_gates(fwd_routes[0], fwd_gates[0], size),
        ],
        axis=1,
    )
    table = jnp.pad(table, ((0, 0), (0, -table.shape[1] % LANES))).astype(BF16)
    places = jnp.stack([me, me + size]).astype(jnp.int32)
    parts = three_ways(size, count)
    first = send(fwd_tokens[0], size, top_bit(size))
    tables = table, send(table, size, top_bit(size))
    pair = [jnp.concatenate(both, axis=1) for both in zip((fwd_tokens[0], first), tables)]
    pair = [jnp.concatenate([p[a:b] for p in pair]) for a, b, _ in parts]
    xf_kept, xf_new = spread_rest(pair, size, parts)
    y_kept = forward_rows(places, xf_kept, w_gu, w_dn, groups)

    def forward_new(xf_new):
        return forward_rows(places, xf_new, w_gu, w_dn, groups)

    def forward_first(y_kept, y_new, *hold):
        return collect_first(y_kept, y_new, size, parts, hold)

    def forward_last(rows):
        return collect_rest(rows, size, parts).astype(BF16)

    xd_in = [
        jnp.concatenate([v[a:b] for v in (bwd_tokens[0], cotangent[0], table)], axis=1)
        for a, b, _ in parts
    ]
    if groups > 1:
        y_new = forward_new(after(xf_new, y_kept))
        combined = forward_last(forward_first(y_kept, y_new))
        xd_in = after(xd_in, combined)
    pair = []
    for k in (1, 2, 0):
        xd_in[k] = after(xd_in[k], first)
        first = send(xd_in[k], size, top_bit(size))
        pair.append(jnp.concatenate([xd_in[k], first]))
    xd_kept, xd_new = spread_rest([pair[2], pair[0], pair[1]], size, parts)
    other_routes = lax.ppermute(bwd_routes[0], "segment", swap)

    if groups == 1:
        y_new = forward_new(after(xf_new, y_kept))
        xd_kept = after(xd_kept, y_new)
    dx_kept, dh_kept, wa_kept = back_rows(places, xd_kept, w_gu, w_dn, groups)
    xd_new = after(xd_new, dx_kept)
    if groups == 1:
        y_new = after(y_new, xd_new)
    dx_new, dh_new, wa_new = back_rows(places, xd_new, w_gu, w_dn, groups)
    if groups == 1:
        comb_rows = forward_first(y_kept, y_new, dx_new)
        dh_kept = after(dh_kept, comb_rows)
    home_rows = collect_first(dx_kept, dx_new, size, parts, ())
    wa_kept = after(wa_kept, home_rows)
    if groups == 1:
        combined = forward_last(comb_rows)
    home = collect_rest(home_rows, size, parts)

    xds = [*xd_kept, *xd_new]
    grad_gu = weight_grad(xds, [dh_kept, dh_new], 0, width, 0, 2 * ff, groups)
    grad_dn = weight_grad([wa_kept, wa_new], xds, 0, ff, width, width, groups)

    token_grad = home[:, :width].astype(BF16)
    hit = other_routes[:, :, None] == jnp.arange(size, dtype=jnp.int32)[None, None, :]
    gate_home = jnp.sum(jnp.where(hit, home[:, None, width : width + size], 0.0), axis=2)
    return (
        combined[None],
        token_grad[None],
        gate_home.astype(BF16)[None],
        grad_gu[None, None],
        grad_dn[None, None],
    )


def solution(mesh):
    three = P("segment", "expert", None)
    four = P("segment", "expert", None, None)

    return jax.shard_map(
        shards,
        mesh=mesh,
        in_specs=(three,) * 7 + (four,) * 2,
        out_specs=(three,) * 3 + (four,) * 2,
        check_vma=False,
    )
```

```python
import jax
import jax.numpy as jnp
from jax import lax
from jax.experimental import pallas as pl
from jax.experimental.pallas import tpu as pltpu
from jax.sharding import PartitionSpec as P


LANES = 128
F32 = jnp.float32
BF16 = jnp.bfloat16
NT = (((1,), (1,)), ((), ()))
TN = (((0,), (0,)), ((), ()))
VMEM_BYTES = 50 << 20
ANY = pl.BlockSpec(memory_space=pl.ANY)


def after(value, *others):
    return lax.optimization_barrier((value, *others))[0]


def send(array, size, bit):
    return lax.ppermute(array, "expert", [(i, i ^ (1 << bit)) for i in range(size)])


def three_ways(size, count):
    bits = size.bit_length() - 1
    middle = list(range(2, bits - 1))
    small, large = count // 4, 3 * count // 8
    return [
        (0, small, [0, 1, *middle]),
        (small, small + large, [1, *middle, 0]),
        (small + large, count, [*middle, 0, 1]),
    ]


def send_all(arrays, size, parts, step):
    bits = [p[2][step] for p in parts]
    got = [None] * len(arrays)
    for bit in dict.fromkeys(bits):
        which = [i for i, b in enumerate(bits) if b == bit]
        whole = send(jnp.concatenate([arrays[i] for i in which]), size, bit)
        start = 0
        for i in which:
            got[i] = whole[start : start + arrays[i].shape[0]]
            start += arrays[i].shape[0]
    return got


def top_bit(size):
    return size.bit_length() - 2


def spread_rest(kept, size, parts):
    for step in range(len(parts[0][2]) - 1):
        got = send_all(kept, size, parts, step)
        kept = [jnp.concatenate([k, g]) for k, g in zip(kept, got)]
    return kept, send_all(kept, size, parts, -1)


def add(a, b):
    return (a.astype(F32) + b.astype(F32)).astype(BF16)


def merge(kept, got):
    n = kept.shape[0] // 2
    return add(kept[:n], got[:n]), add(kept[n:], got[n:])


def collect_first(kept, away, size, parts, hold):
    got = after(send_all(away, size, parts, -1), *hold)
    return [merge(k, g) for k, g in zip(kept, got)]


def collect_rest(rows, size, parts):
    for step in range(len(parts[0][2]) - 2, -1, -1):
        got = send_all([r[1] for r in rows], size, parts, step)
        rows = [merge(r[0], g) for r, g in zip(rows, got)]
    sections = lax.axis_size("segment")
    cross = lambda flip: [
        (s * size + i, (s ^ 1) * size + (i ^ flip)) for s in range(sections) for i in range(size)
    ]
    own, other = (jnp.concatenate([r[k] for r in rows]) for k in range(2))
    other = lax.ppermute(other, ("segment", "expert"), cross(size // 2))
    own = lax.ppermute(own, ("segment", "expert"), cross(0))
    return own.astype(F32) + other.astype(F32)


def dense_gates(routes, gates, size):
    hit = routes[:, :, None] == jnp.arange(size, dtype=jnp.int32)[None, None, :]
    return jnp.sum(jnp.where(hit, gates[:, :, None].astype(F32), 0.0), axis=1)


def pick(table, at):
    lane = lax.broadcasted_iota(jnp.int32, table.shape, 1)
    return jnp.sum(jnp.where(lane == at, table.astype(F32), 0.0), axis=1, keepdims=True)


def copies_of(pairs, sems, start):
    return [pltpu.make_async_copy(a, b, sems.at[start + i]) for i, (a, b) in enumerate(pairs)]


def begin(made):
    for copy in made:
        copy.start()


def end(made):
    for copy in made:
        copy.wait()


def starts_of(counts):
    return [sum(counts[:i]) for i in range(len(counts))]


def block_start(step, count):
    return step * count if isinstance(step, int) else pl.multiple_of(step * count, 8)


def span(at, count):
    return pl.ds(at if isinstance(at, int) else pl.multiple_of(at, LANES), count)


def row_pairs(pieces, whole, counts, step, at, columns, outward=False):
    pairs = []
    for piece, count, start in zip(pieces, counts, starts_of(counts)):
        outer = piece.at[pl.ds(block_start(step, count), count), span(at, columns)]
        inner = whole.at[pl.ds(start, count)]
        pairs.append((inner, outer) if outward else (outer, inner))
    return pairs


def once(groups, step):
    return pl.when(step == 0) if groups > 1 else lambda run: run()


CHUNKS = 3
PANELS = 4


def weight_copies(wgu_ref, wdn_ref, wgu, wdn, sems, j):
    ff = wdn.shape[0]
    wide = ff // CHUNKS
    pairs = [(wgu_ref.at[:, span(at, wide)], wgu.at[:, span(at, wide)]) for at in (j * wide, ff + j * wide)]
    rows = span(j * wide, wide)
    pairs.append((wdn_ref.at[rows], wdn.at[rows]))
    return copies_of(pairs, sems, 3 * j)


def back_kernel(counts, groups, me_ref, *refs):
    n = len(counts)
    xd_in, (wgu_ref, wdn_ref) = refs[:n], refs[n : n + 2]
    dx_out, (dh_out, wa_out) = refs[n + 2 : 2 * n + 2], refs[2 * n + 2 : 2 * n + 4]
    x, dy, table, wgu, wdn, dx, extra, dh, wa, gate_grad, sems, w_sems, out_sems = refs[2 * n + 4 :]
    me = me_ref[0]
    step = pl.program_id(0) if groups > 1 else 0
    ff, width = wdn.shape
    lanes = table.shape[1]
    rows = x.shape[0]
    weights = lambda j: weight_copies(wgu_ref, wdn_ref, wgu, wdn, w_sems, j)
    first = once(groups, step)
    ins = copies_of(row_pairs(xd_in, x, counts, step, 0, width), sems, 0)
    dys = copies_of(
        row_pairs(xd_in, dy, counts, step, width, width)
        + row_pairs(xd_in, table, counts, step, 2 * width, lanes),
        sems,
        n,
    )
    begin(ins)
    first(lambda: begin(weights(0)))
    begin(dys)

    @first
    def _():
        for j in range(1, CHUNKS):
            begin(weights(j))

    end(ins)
    end(dys)
    wide = ff // CHUNKS
    gate_grad[...] = jnp.zeros_like(gate_grad)

    @pl.loop(0, CHUNKS)
    def _(j):
        first(lambda: end(weights(j)))
        own = span(j * wide, wide)
        also = span(ff + j * wide, wide)
        gate = jnp.dot(x[...], wgu[:, own], preferred_element_type=F32)
        upper = jnp.dot(x[...], wgu[:, also], preferred_element_type=F32)
        back = lax.dot_general(dy[...], wdn[own], NT, preferred_element_type=F32)
        gate_b = pick(table[...], me)
        sigma = jax.nn.sigmoid(gate)
        silu = gate * sigma
        active = silu * upper
        gate_grad[...] += jnp.sum(active * back, axis=1, keepdims=True)
        wa[:, own] = (active * gate_b).astype(BF16)
        d_active = back * gate_b
        dh[:, own] = (d_active * upper * sigma * (1.0 + gate * (1.0 - sigma))).astype(BF16)
        dh[:, also] = (d_active * silu).astype(BF16)

    lane = lax.broadcasted_iota(jnp.int32, (rows, lanes), 1)
    extra[...] = jnp.where(lane == me, gate_grad[...], 0.0).astype(BF16)
    here = pl.ds(block_start(step, rows), rows)
    outs = copies_of(
        row_pairs(dx_out, extra, counts, step, width, lanes, True)
        + [(dh, dh_out.at[here]), (wa, wa_out.at[here])],
        sems,
        3 * n,
    )
    begin(outs)
    panel = width // PANELS

    def panel_copies(p):
        pairs = row_pairs(dx_out, dx.at[p], counts, step, p * panel, panel, True)
        return copies_of(pairs, out_sems, n * p)

    @pl.loop(0, PANELS)
    def _(p):
        dx[p] = lax.dot_general(
            dh[...], wgu[span(p * panel, panel)], NT, preferred_element_type=F32
        ).astype(BF16)
        begin(panel_copies(p))

    end(outs)
    for p in range(PANELS):
        end(panel_copies(p))


def group_counts(pieces, groups):
    return [p.shape[0] // groups for p in pieces]


def back_rows(me, xds, w_gu, w_dn, groups):
    ff, width = w_dn.shape
    lanes = xds[0].shape[1] - 2 * width
    counts = group_counts(xds, groups)
    rows = sum(counts)
    n = len(counts)
    total = rows * groups
    shape = jax.ShapeDtypeStruct
    out = pl.pallas_call(
        lambda *refs: back_kernel(counts, groups, *refs),
        grid_spec=pltpu.PrefetchScalarGridSpec(
            num_scalar_prefetch=1,
            grid=(groups,),
            in_specs=[ANY] * (n + 2),
            out_specs=[ANY] * (n + 2),
            scratch_shapes=[
                pltpu.VMEM((rows, width), BF16),
                pltpu.VMEM((rows, width), BF16),
                pltpu.VMEM((rows, lanes), BF16),
                pltpu.VMEM(w_gu.shape, BF16),
                pltpu.VMEM(w_dn.shape, BF16),
                pltpu.VMEM((PANELS, rows, width // PANELS), BF16),
                pltpu.VMEM((rows, lanes), BF16),
                pltpu.VMEM((rows, 2 * ff), BF16),
                pltpu.VMEM((rows, ff), BF16),
                pltpu.VMEM((rows, 1), F32),
                pltpu.SemaphoreType.DMA((4 * n + 2,)),
                pltpu.SemaphoreType.DMA((3 * CHUNKS,)),
                pltpu.SemaphoreType.DMA((n * PANELS,)),
            ],
        ),
        out_shape=[shape((p.shape[0], width + lanes), BF16) for p in xds]
        + [shape((total, 2 * ff), BF16), shape((total, ff), BF16)],
        compiler_params=pltpu.CompilerParams(vmem_limit_bytes=VMEM_BYTES),
        cost_estimate=pl.CostEstimate(
            flops=total * width * ff * 10,
            bytes_accessed=6 * ff * width + total * (6 * width + 4 * lanes + 6 * ff),
            transcendentals=total * ff,
        ),
    )(me, *xds, w_gu, w_dn)
    return out[:n], out[n], out[n + 1]


def forward_kernel(counts, groups, me_ref, *refs):
    n = len(counts)
    x_in, (wgu_ref, wdn_ref), y_out = refs[:n], refs[n : n + 2], refs[n + 2 : 2 * n + 2]
    x, table, wgu, wdn, act, y, sems, w_sems, out_sems = refs[2 * n + 2 :]
    step = pl.program_id(0) if groups > 1 else 0
    ff, width = wdn.shape
    lanes = table.shape[1]
    weights = lambda j: weight_copies(wgu_ref, wdn_ref, wgu, wdn, w_sems, j)
    first = once(groups, step)
    ins = copies_of(
        row_pairs(x_in, x, counts, step, 0, width)
        + row_pairs(x_in, table, counts, step, width, lanes),
        sems,
        0,
    )
    begin(ins)

    @first
    def _():
        for j in range(CHUNKS):
            begin(weights(j))

    end(ins)
    wide = ff // CHUNKS

    @pl.loop(0, CHUNKS)
    def _(j):
        first(lambda: end(weights(j)))
        own = span(j * wide, wide)
        also = span(ff + j * wide, wide)
        gate = jnp.dot(x[...], wgu[:, own], preferred_element_type=F32)
        upper = jnp.dot(x[...], wgu[:, also], preferred_element_type=F32)
        act[:, own] = (gate * jax.nn.sigmoid(gate) * upper).astype(BF16)

    panel = width // PANELS

    def panel_copies(p):
        pairs = row_pairs(y_out, y.at[p], counts, step, p * panel, panel, True)
        return copies_of(pairs, out_sems, n * p)

    @pl.loop(0, PANELS)
    def _(p):
        gate_f = pick(table[...], me_ref[1])
        cols = span(p * panel, panel)
        y[p] = (jnp.dot(act[...], wdn[:, cols], preferred_element_type=F32) * gate_f).astype(BF16)
        begin(panel_copies(p))

    for p in range(PANELS):
        end(panel_copies(p))


def forward_rows(me, xs, w_gu, w_dn, groups):
    ff, width = w_dn.shape
    lanes = xs[0].shape[1] - width
    counts = group_counts(xs, groups)
    rows = sum(counts)
    n = len(counts)
    total = rows * groups
    return pl.pallas_call(
        lambda *refs: forward_kernel(counts, groups, *refs),
        grid_spec=pltpu.PrefetchScalarGridSpec(
            num_scalar_prefetch=1,
            grid=(groups,),
            in_specs=[ANY] * (n + 2),
            out_specs=[ANY] * n,
            scratch_shapes=[
                pltpu.VMEM((rows, width), BF16),
                pltpu.VMEM((rows, lanes), BF16),
                pltpu.VMEM(w_gu.shape, BF16),
                pltpu.VMEM(w_dn.shape, BF16),
                pltpu.VMEM((rows, ff), BF16),
                pltpu.VMEM((PANELS, rows, width // PANELS), BF16),
                pltpu.SemaphoreType.DMA((2 * n,)),
                pltpu.SemaphoreType.DMA((3 * CHUNKS,)),
                pltpu.SemaphoreType.DMA((n * PANELS,)),
            ],
        ),
        out_shape=[jax.ShapeDtypeStruct((p.shape[0], width), BF16) for p in xs],
        compiler_params=pltpu.CompilerParams(vmem_limit_bytes=VMEM_BYTES),
        cost_estimate=pl.CostEstimate(
            flops=total * width * ff * 6,
            bytes_accessed=6 * ff * width + total * 4 * width,
            transcendentals=total * ff,
        ),
    )(me, *xs, w_gu, w_dn)


def weight_kernel(lefts, rights, left_at, right_at, groups, *refs):
    n, m = len(lefts), len(rights)
    left_in, right_in, out_ref = refs[:n], refs[n : n + m], refs[n + m]
    left, right, stage = refs[n + m + 1 : n + m + 4]
    sems, left_sems, out_sems = refs[-3:]
    step = pl.program_id(0) if groups > 1 else 0
    tiles, _, tile = left.shape
    rights_made = copies_of(row_pairs(right_in, right, rights, step, right_at, right.shape[1]), sems, 0)
    begin(rights_made)

    def left_copies(t):
        pairs = row_pairs(left_in, left.at[t], lefts, step, left_at + t * tile, tile)
        return copies_of(pairs, left_sems, n * t)

    def out_copy(t):
        return copies_of([(stage.at[t], out_ref.at[span(t * tile, tile)])], out_sems, t)

    for t in range(tiles):
        begin(left_copies(t))
    end(rights_made)

    @pl.loop(0, tiles)
    def _(t):
        end(left_copies(t))
        part = lax.dot_general(left[t], right[...], TN, preferred_element_type=F32)
        if groups > 1:
            total = refs[n + m + 4]
            part += jnp.where(step == 0, 0.0, total[t])
            total[t] = part
            stage[t] = part.astype(BF16)
            pl.when(step == groups - 1)(lambda: begin(out_copy(t)))
        else:
            stage[t] = part.astype(BF16)
            begin(out_copy(t))

    def finish():
        for t in range(tiles):
            end(out_copy(t))

    pl.when(step == groups - 1)(finish) if groups > 1 else finish()


def weight_grad(lefts, rights, left_at, left_wide, right_at, right_wide, groups):
    left_counts = group_counts(lefts, groups)
    right_counts = group_counts(rights, groups)
    rows = sum(left_counts)
    tile = 256
    tiles = left_wide // tile
    scratch = [
        pltpu.VMEM((tiles, rows, tile), BF16),
        pltpu.VMEM((rows, right_wide), BF16),
        pltpu.VMEM((tiles, tile, right_wide), BF16),
    ]
    if groups > 1:
        scratch.append(pltpu.VMEM((tiles, tile, right_wide), F32))
    scratch += [pltpu.SemaphoreType.DMA((k,)) for k in (len(rights), tiles * len(lefts), tiles)]
    return pl.pallas_call(
        lambda *refs: weight_kernel(left_counts, right_counts, left_at, right_at, groups, *refs),
        grid=(groups,),
        in_specs=[ANY] * (len(lefts) + len(rights)),
        out_specs=ANY,
        out_shape=jax.ShapeDtypeStruct((left_wide, right_wide), BF16),
        scratch_shapes=scratch,
        compiler_params=pltpu.CompilerParams(vmem_limit_bytes=VMEM_BYTES),
        cost_estimate=pl.CostEstimate(
            flops=2 * rows * groups * left_wide * right_wide,
            bytes_accessed=2 * rows * groups * (left_wide + right_wide) + 2 * left_wide * right_wide,
            transcendentals=0,
        ),
    )(*lefts, *rights)


def shards(
    fwd_tokens,
    fwd_routes,
    fwd_gates,
    bwd_tokens,
    bwd_routes,
    bwd_gates,
    cotangent,
    w_gate_up,
    w_down,
):
    size = lax.axis_size("expert")
    me = lax.axis_index("expert")
    count, width = fwd_tokens.shape[1:]
    w_gu = w_gate_up[0, 0]
    w_dn = w_down[0, 0]
    ff = w_dn.shape[0]
    groups = max(1, size // 16)
    sections = lax.axis_size("segment")
    swap = [(s, s ^ 1) for s in range(sections)]
    table = jnp.concatenate(
        [
            dense_gates(bwd_routes[0], bwd_gates[0], size),
            dense_gates(fwd_routes[0], fwd_gates[0], size),
        ],
        axis=1,
    )
    table = jnp.pad(table, ((0, 0), (0, -table.shape[1] % LANES))).astype(BF16)
    places = jnp.stack([me, me + size]).astype(jnp.int32)
    parts = three_ways(size, count)
    first = send(fwd_tokens[0], size, top_bit(size))
    tables = table, send(table, size, top_bit(size))
    pair = [jnp.concatenate(both, axis=1) for both in zip((fwd_tokens[0], first), tables)]
    pair = [jnp.concatenate([p[a:b] for p in pair]) for a, b, _ in parts]
    xf_kept, xf_new = spread_rest(pair, size, parts)
    y_kept = forward_rows(places, xf_kept, w_gu, w_dn, groups)

    def forward_new(xf_new):
        return forward_rows(places, xf_new, w_gu, w_dn, groups)

    def forward_first(y_kept, y_new, *hold):
        return collect_first(y_kept, y_new, size, parts, hold)

    def forward_last(rows):
        return collect_rest(rows, size, parts).astype(BF16)

    xd_in = jnp.concatenate([bwd_tokens[0], cotangent[0], table], axis=1)
    if groups > 1:
        y_new = forward_new(after(xf_new, y_kept))
        combined = forward_last(forward_first(y_kept, y_new))
        xd_in = after(xd_in, combined)
    xd_in = after(xd_in, first)
    pair = xd_in, send(xd_in, size, top_bit(size))
    pair = [jnp.concatenate([p[a:b] for p in pair]) for a, b, _ in parts]
    xd_kept, xd_new = spread_rest(pair, size, parts)
    other_routes = lax.ppermute(bwd_routes[0], "segment", swap)

    if groups == 1:
        y_new = forward_new(after(xf_new, y_kept))
        xd_kept = after(xd_kept, y_new)
    dx_kept, dh_kept, wa_kept = back_rows(places, xd_kept, w_gu, w_dn, groups)
    xd_new = after(xd_new, dx_kept)
    if groups == 1:
        y_new = after(y_new, xd_new)
    dx_new, dh_new, wa_new = back_rows(places, xd_new, w_gu, w_dn, groups)
    if groups == 1:
        comb_rows = forward_first(y_kept, y_new, dx_new)
        wa_kept = after(wa_kept, comb_rows)
    home_rows = collect_first(dx_kept, dx_new, size, parts, ())
    if groups == 1:
        combined = forward_last(comb_rows)
    home = collect_rest(home_rows, size, parts)

    xds = [*xd_kept, *xd_new]
    grad_gu = weight_grad(xds, [dh_kept, dh_new], 0, width, 0, 2 * ff, groups)
    grad_dn = weight_grad([wa_kept, wa_new], xds, 0, ff, width, width, groups)

    token_grad = home[:, :width].astype(BF16)
    hit = other_routes[:, :, None] == jnp.arange(size, dtype=jnp.int32)[None, None, :]
    gate_home = jnp.sum(jnp.where(hit, home[:, None, width : width + size], 0.0), axis=2)
    return (
        combined[None],
        token_grad[None],
        gate_home.astype(BF16)[None],
        grad_gu[None, None],
        grad_dn[None, None],
    )


def solution(mesh):
    three = P("segment", "expert", None)
    four = P("segment", "expert", None, None)

    return jax.shard_map(
        shards,
        mesh=mesh,
        in_specs=(three,) * 7 + (four,) * 2,
        out_specs=(three,) * 3 + (four,) * 2,
        check_vma=False,
    )
```

```python
import jax
import jax.numpy as jnp
from jax import lax
from jax.experimental import pallas as pl
from jax.experimental.pallas import tpu as pltpu
from jax.sharding import PartitionSpec as P


LANES = 128
F32 = jnp.float32
BF16 = jnp.bfloat16
NT = (((1,), (1,)), ((), ()))
TN = (((0,), (0,)), ((), ()))
VMEM_BYTES = 50 << 20
ANY = pl.BlockSpec(memory_space=pl.ANY)


def after(value, *others):
    return lax.optimization_barrier((value, *others))[0]


def send(array, size, bit):
    return lax.ppermute(array, "expert", [(i, i ^ (1 << bit)) for i in range(size)])


def three_ways(size, count):
    bits = size.bit_length() - 1
    middle = list(range(2, bits - 1))
    small, large = count // 4, 3 * count // 8
    return [
        (0, small, [0, 1, *middle]),
        (small, small + large, [1, *middle, 0]),
        (small + large, count, [*middle, 0, 1]),
    ]


def send_all(arrays, size, parts, step):
    bits = [p[2][step] for p in parts]
    got = [None] * len(arrays)
    for bit in dict.fromkeys(bits):
        which = [i for i, b in enumerate(bits) if b == bit]
        whole = send(jnp.concatenate([arrays[i] for i in which]), size, bit)
        start = 0
        for i in which:
            got[i] = whole[start : start + arrays[i].shape[0]]
            start += arrays[i].shape[0]
    return got


def top_bit(size):
    return size.bit_length() - 2


def spread_rest(kept, size, parts):
    for step in range(len(parts[0][2]) - 1):
        got = send_all(kept, size, parts, step)
        kept = [jnp.concatenate([k, g]) for k, g in zip(kept, got)]
    return kept, send_all(kept, size, parts, -1)


def add(a, b):
    return (a.astype(F32) + b.astype(F32)).astype(BF16)


def merge(kept, got):
    n = kept.shape[0] // 2
    return add(kept[:n], got[:n]), add(kept[n:], got[n:])


def collect_first(kept, away, size, parts, hold):
    got = after(send_all(away, size, parts, -1), *hold)
    return [merge(k, g) for k, g in zip(kept, got)]


def collect_rest(rows, size, parts):
    for step in range(len(parts[0][2]) - 2, -1, -1):
        got = send_all([r[1] for r in rows], size, parts, step)
        rows = [merge(r[0], g) for r, g in zip(rows, got)]
    sections = lax.axis_size("segment")
    cross = lambda flip: [
        (s * size + i, (s ^ 1) * size + (i ^ flip)) for s in range(sections) for i in range(size)
    ]
    own, other = (jnp.concatenate([r[k] for r in rows]) for k in range(2))
    other = lax.ppermute(other, ("segment", "expert"), cross(size // 2))
    own = lax.ppermute(own, ("segment", "expert"), cross(0))
    return own.astype(F32) + other.astype(F32)


def dense_gates(routes, gates, size):
    hit = routes[:, :, None] == jnp.arange(size, dtype=jnp.int32)[None, None, :]
    return jnp.sum(jnp.where(hit, gates[:, :, None].astype(F32), 0.0), axis=1)


def pick(table, at):
    lane = lax.broadcasted_iota(jnp.int32, table.shape, 1)
    return jnp.sum(jnp.where(lane == at, table.astype(F32), 0.0), axis=1, keepdims=True)


def copies_of(pairs, sems, start):
    return [pltpu.make_async_copy(a, b, sems.at[start + i]) for i, (a, b) in enumerate(pairs)]


def begin(made):
    for copy in made:
        copy.start()


def end(made):
    for copy in made:
        copy.wait()


def starts_of(counts):
    return [sum(counts[:i]) for i in range(len(counts))]


def block_start(step, count):
    return step * count if isinstance(step, int) else pl.multiple_of(step * count, 8)


def span(at, count):
    return pl.ds(at if isinstance(at, int) else pl.multiple_of(at, LANES), count)


def row_pairs(pieces, whole, counts, step, at, columns, outward=False):
    pairs = []
    for piece, count, start in zip(pieces, counts, starts_of(counts)):
        outer = piece.at[pl.ds(block_start(step, count), count), span(at, columns)]
        inner = whole.at[pl.ds(start, count)]
        pairs.append((inner, outer) if outward else (outer, inner))
    return pairs


def once(groups, step):
    return pl.when(step == 0) if groups > 1 else lambda run: run()


CHUNKS = 3
PANELS = 4


def weight_copies(wgu_ref, wdn_ref, wgu, wdn, sems, j):
    ff = wdn.shape[0]
    wide = ff // CHUNKS
    pairs = [(wgu_ref.at[:, span(at, wide)], wgu.at[:, span(at, wide)]) for at in (j * wide, ff + j * wide)]
    rows = span(j * wide, wide)
    pairs.append((wdn_ref.at[rows], wdn.at[rows]))
    return copies_of(pairs, sems, 3 * j)


def back_kernel(counts, groups, me_ref, *refs):
    n = len(counts)
    xd_in, tables, (wgu_ref, wdn_ref) = refs[:n], refs[n : 2 * n], refs[2 * n : 2 * n + 2]
    dx_out, (dh_out, wa_out) = refs[2 * n + 2 : 3 * n + 2], refs[3 * n + 2 : 3 * n + 4]
    x, dy, table, wgu, wdn, dx, extra, dh, wa, gate_grad, sems, w_sems, out_sems = refs[3 * n + 4 :]
    me = me_ref[0]
    step = pl.program_id(0) if groups > 1 else 0
    ff, width = wdn.shape
    lanes = table.shape[1]
    rows = x.shape[0]
    weights = lambda j: weight_copies(wgu_ref, wdn_ref, wgu, wdn, w_sems, j)
    first = once(groups, step)
    ins = copies_of(row_pairs(xd_in, x, counts, step, 0, width), sems, 0)
    dys = copies_of(
        row_pairs(xd_in, dy, counts, step, width, width)
        + row_pairs(tables, table, counts, step, width, lanes),
        sems,
        n,
    )
    begin(ins)
    first(lambda: begin(weights(0)))
    begin(dys)

    @first
    def _():
        for j in range(1, CHUNKS):
            begin(weights(j))

    end(ins)
    end(dys)
    wide = ff // CHUNKS
    gate_grad[...] = jnp.zeros_like(gate_grad)

    @pl.loop(0, CHUNKS)
    def _(j):
        first(lambda: end(weights(j)))
        own = span(j * wide, wide)
        also = span(ff + j * wide, wide)
        gate = jnp.dot(x[...], wgu[:, own], preferred_element_type=F32)
        upper = jnp.dot(x[...], wgu[:, also], preferred_element_type=F32)
        back = lax.dot_general(dy[...], wdn[own], NT, preferred_element_type=F32)
        gate_b = pick(table[...], me)
        sigma = jax.nn.sigmoid(gate)
        silu = gate * sigma
        active = silu * upper
        gate_grad[...] += jnp.sum(active * back, axis=1, keepdims=True)
        wa[:, own] = (active * gate_b).astype(BF16)
        d_active = back * gate_b
        dh[:, own] = (d_active * upper * sigma * (1.0 + gate * (1.0 - sigma))).astype(BF16)
        dh[:, also] = (d_active * silu).astype(BF16)

    lane = lax.broadcasted_iota(jnp.int32, (rows, lanes), 1)
    extra[...] = jnp.where(lane == me, gate_grad[...], 0.0).astype(BF16)
    here = pl.ds(block_start(step, rows), rows)
    outs = copies_of(
        row_pairs(dx_out, extra, counts, step, width, lanes, True)
        + [(dh, dh_out.at[here]), (wa, wa_out.at[here])],
        sems,
        3 * n,
    )
    begin(outs)
    panel = width // PANELS

    def panel_copies(p):
        pairs = row_pairs(dx_out, dx.at[p], counts, step, p * panel, panel, True)
        return copies_of(pairs, out_sems, n * p)

    @pl.loop(0, PANELS)
    def _(p):
        dx[p] = lax.dot_general(
            dh[...], wgu[span(p * panel, panel)], NT, preferred_element_type=F32
        ).astype(BF16)
        begin(panel_copies(p))

    end(outs)
    for p in range(PANELS):
        end(panel_copies(p))


def group_counts(pieces, groups):
    return [p.shape[0] // groups for p in pieces]


def back_rows(me, xds, tables, w_gu, w_dn, groups):
    ff, width = w_dn.shape
    lanes = tables[0].shape[1] - width
    counts = group_counts(xds, groups)
    rows = sum(counts)
    n = len(counts)
    total = rows * groups
    shape = jax.ShapeDtypeStruct
    out = pl.pallas_call(
        lambda *refs: back_kernel(counts, groups, *refs),
        grid_spec=pltpu.PrefetchScalarGridSpec(
            num_scalar_prefetch=1,
            grid=(groups,),
            in_specs=[ANY] * (2 * n + 2),
            out_specs=[ANY] * (n + 2),
            scratch_shapes=[
                pltpu.VMEM((rows, width), BF16),
                pltpu.VMEM((rows, width), BF16),
                pltpu.VMEM((rows, lanes), BF16),
                pltpu.VMEM(w_gu.shape, BF16),
                pltpu.VMEM(w_dn.shape, BF16),
                pltpu.VMEM((PANELS, rows, width // PANELS), BF16),
                pltpu.VMEM((rows, lanes), BF16),
                pltpu.VMEM((rows, 2 * ff), BF16),
                pltpu.VMEM((rows, ff), BF16),
                pltpu.VMEM((rows, 1), F32),
                pltpu.SemaphoreType.DMA((4 * n + 2,)),
                pltpu.SemaphoreType.DMA((3 * CHUNKS,)),
                pltpu.SemaphoreType.DMA((n * PANELS,)),
            ],
        ),
        out_shape=[shape((p.shape[0], width + lanes), BF16) for p in xds]
        + [shape((total, 2 * ff), BF16), shape((total, ff), BF16)],
        compiler_params=pltpu.CompilerParams(vmem_limit_bytes=VMEM_BYTES),
        cost_estimate=pl.CostEstimate(
            flops=total * width * ff * 10,
            bytes_accessed=6 * ff * width + total * (6 * width + 4 * lanes + 6 * ff),
            transcendentals=total * ff,
        ),
    )(me, *xds, *tables, w_gu, w_dn)
    return out[:n], out[n], out[n + 1]


def forward_kernel(counts, groups, me_ref, *refs):
    n = len(counts)
    x_in, (wgu_ref, wdn_ref), y_out = refs[:n], refs[n : n + 2], refs[n + 2 : 2 * n + 2]
    x, table, wgu, wdn, act, y, sems, w_sems, out_sems = refs[2 * n + 2 :]
    step = pl.program_id(0) if groups > 1 else 0
    ff, width = wdn.shape
    lanes = table.shape[1]
    weights = lambda j: weight_copies(wgu_ref, wdn_ref, wgu, wdn, w_sems, j)
    first = once(groups, step)
    ins = copies_of(
        row_pairs(x_in, x, counts, step, 0, width)
        + row_pairs(x_in, table, counts, step, width, lanes),
        sems,
        0,
    )
    begin(ins)

    @first
    def _():
        for j in range(CHUNKS):
            begin(weights(j))

    end(ins)
    wide = ff // CHUNKS

    @pl.loop(0, CHUNKS)
    def _(j):
        first(lambda: end(weights(j)))
        own = span(j * wide, wide)
        also = span(ff + j * wide, wide)
        gate = jnp.dot(x[...], wgu[:, own], preferred_element_type=F32)
        upper = jnp.dot(x[...], wgu[:, also], preferred_element_type=F32)
        act[:, own] = (gate * jax.nn.sigmoid(gate) * upper).astype(BF16)

    panel = width // PANELS

    def panel_copies(p):
        pairs = row_pairs(y_out, y.at[p], counts, step, p * panel, panel, True)
        return copies_of(pairs, out_sems, n * p)

    @pl.loop(0, PANELS)
    def _(p):
        gate_f = pick(table[...], me_ref[1])
        cols = span(p * panel, panel)
        y[p] = (jnp.dot(act[...], wdn[:, cols], preferred_element_type=F32) * gate_f).astype(BF16)
        begin(panel_copies(p))

    for p in range(PANELS):
        end(panel_copies(p))


def forward_rows(me, xs, w_gu, w_dn, groups):
    ff, width = w_dn.shape
    lanes = xs[0].shape[1] - width
    counts = group_counts(xs, groups)
    rows = sum(counts)
    n = len(counts)
    total = rows * groups
    return pl.pallas_call(
        lambda *refs: forward_kernel(counts, groups, *refs),
        grid_spec=pltpu.PrefetchScalarGridSpec(
            num_scalar_prefetch=1,
            grid=(groups,),
            in_specs=[ANY] * (n + 2),
            out_specs=[ANY] * n,
            scratch_shapes=[
                pltpu.VMEM((rows, width), BF16),
                pltpu.VMEM((rows, lanes), BF16),
                pltpu.VMEM(w_gu.shape, BF16),
                pltpu.VMEM(w_dn.shape, BF16),
                pltpu.VMEM((rows, ff), BF16),
                pltpu.VMEM((PANELS, rows, width // PANELS), BF16),
                pltpu.SemaphoreType.DMA((2 * n,)),
                pltpu.SemaphoreType.DMA((3 * CHUNKS,)),
                pltpu.SemaphoreType.DMA((n * PANELS,)),
            ],
        ),
        out_shape=[jax.ShapeDtypeStruct((p.shape[0], width), BF16) for p in xs],
        compiler_params=pltpu.CompilerParams(vmem_limit_bytes=VMEM_BYTES),
        cost_estimate=pl.CostEstimate(
            flops=total * width * ff * 6,
            bytes_accessed=6 * ff * width + total * 4 * width,
            transcendentals=total * ff,
        ),
    )(me, *xs, w_gu, w_dn)


def weight_kernel(lefts, rights, left_at, right_at, groups, *refs):
    n, m = len(lefts), len(rights)
    left_in, right_in, out_ref = refs[:n], refs[n : n + m], refs[n + m]
    left, right, stage = refs[n + m + 1 : n + m + 4]
    sems, left_sems, out_sems = refs[-3:]
    step = pl.program_id(0) if groups > 1 else 0
    tiles, _, tile = left.shape
    rights_made = copies_of(row_pairs(right_in, right, rights, step, right_at, right.shape[1]), sems, 0)
    begin(rights_made)

    def left_copies(t):
        pairs = row_pairs(left_in, left.at[t], lefts, step, left_at + t * tile, tile)
        return copies_of(pairs, left_sems, n * t)

    def out_copy(t):
        return copies_of([(stage.at[t], out_ref.at[span(t * tile, tile)])], out_sems, t)

    for t in range(tiles):
        begin(left_copies(t))
    end(rights_made)

    @pl.loop(0, tiles)
    def _(t):
        end(left_copies(t))
        part = lax.dot_general(left[t], right[...], TN, preferred_element_type=F32)
        if groups > 1:
            total = refs[n + m + 4]
            part += jnp.where(step == 0, 0.0, total[t])
            total[t] = part
            stage[t] = part.astype(BF16)
            pl.when(step == groups - 1)(lambda: begin(out_copy(t)))
        else:
            stage[t] = part.astype(BF16)
            begin(out_copy(t))

    def finish():
        for t in range(tiles):
            end(out_copy(t))

    pl.when(step == groups - 1)(finish) if groups > 1 else finish()


def weight_grad(lefts, rights, left_at, left_wide, right_at, right_wide, groups):
    left_counts = group_counts(lefts, groups)
    right_counts = group_counts(rights, groups)
    rows = sum(left_counts)
    tile = 256
    tiles = left_wide // tile
    scratch = [
        pltpu.VMEM((tiles, rows, tile), BF16),
        pltpu.VMEM((rows, right_wide), BF16),
        pltpu.VMEM((tiles, tile, right_wide), BF16),
    ]
    if groups > 1:
        scratch.append(pltpu.VMEM((tiles, tile, right_wide), F32))
    scratch += [pltpu.SemaphoreType.DMA((k,)) for k in (len(rights), tiles * len(lefts), tiles)]
    return pl.pallas_call(
        lambda *refs: weight_kernel(left_counts, right_counts, left_at, right_at, groups, *refs),
        grid=(groups,),
        in_specs=[ANY] * (len(lefts) + len(rights)),
        out_specs=ANY,
        out_shape=jax.ShapeDtypeStruct((left_wide, right_wide), BF16),
        scratch_shapes=scratch,
        compiler_params=pltpu.CompilerParams(vmem_limit_bytes=VMEM_BYTES),
        cost_estimate=pl.CostEstimate(
            flops=2 * rows * groups * left_wide * right_wide,
            bytes_accessed=2 * rows * groups * (left_wide + right_wide) + 2 * left_wide * right_wide,
            transcendentals=0,
        ),
    )(*lefts, *rights)


def shards(
    fwd_tokens,
    fwd_routes,
    fwd_gates,
    bwd_tokens,
    bwd_routes,
    bwd_gates,
    cotangent,
    w_gate_up,
    w_down,
):
    size = lax.axis_size("expert")
    me = lax.axis_index("expert")
    count, width = fwd_tokens.shape[1:]
    w_gu = w_gate_up[0, 0]
    w_dn = w_down[0, 0]
    ff = w_dn.shape[0]
    groups = max(1, size // 16)
    sections = lax.axis_size("segment")
    swap = [(s, s ^ 1) for s in range(sections)]
    table = jnp.concatenate(
        [
            dense_gates(bwd_routes[0], bwd_gates[0], size),
            dense_gates(fwd_routes[0], fwd_gates[0], size),
        ],
        axis=1,
    )
    table = jnp.pad(table, ((0, 0), (0, -table.shape[1] % LANES))).astype(BF16)
    places = jnp.stack([me, me + size]).astype(jnp.int32)
    parts = three_ways(size, count)
    first = send(fwd_tokens[0], size, top_bit(size))
    tables = table, send(table, size, top_bit(size))
    pair = [jnp.concatenate(both, axis=1) for both in zip((fwd_tokens[0], first), tables)]
    pair = [jnp.concatenate([p[a:b] for p in pair]) for a, b, _ in parts]
    xf_kept, xf_new = spread_rest(pair, size, parts)
    y_kept = forward_rows(places, xf_kept, w_gu, w_dn, groups)

    def forward_new(xf_new):
        return forward_rows(places, xf_new, w_gu, w_dn, groups)

    def forward_first(y_kept, y_new, *hold):
        return collect_first(y_kept, y_new, size, parts, hold)

    def forward_last(rows):
        return collect_rest(rows, size, parts).astype(BF16)

    xd_in = jnp.concatenate([bwd_tokens[0], cotangent[0]], axis=1)
    if groups > 1:
        y_new = forward_new(after(xf_new, y_kept))
        combined = forward_last(forward_first(y_kept, y_new))
        xd_in = after(xd_in, combined)
    xd_in = after(xd_in, first)
    pair = xd_in, send(xd_in, size, top_bit(size))
    pair = [jnp.concatenate([p[a:b] for p in pair]) for a, b, _ in parts]
    xd_kept, xd_new = spread_rest(pair, size, parts)
    other_routes = lax.ppermute(bwd_routes[0], "segment", swap)

    if groups == 1:
        y_new = forward_new(after(xf_new, y_kept))
        xd_kept = after(xd_kept, y_new)
    dx_kept, dh_kept, wa_kept = back_rows(places, xd_kept, xf_kept, w_gu, w_dn, groups)
    xd_new = after(xd_new, dx_kept)
    if groups == 1:
        y_new = after(y_new, xd_new)
    dx_new, dh_new, wa_new = back_rows(places, xd_new, xf_new, w_gu, w_dn, groups)
    if groups == 1:
        comb_rows = forward_first(y_kept, y_new, dx_new)
        wa_kept = after(wa_kept, comb_rows)
    home_rows = collect_first(dx_kept, dx_new, size, parts, ())
    if groups == 1:
        combined = forward_last(comb_rows)
    home = collect_rest(home_rows, size, parts)

    xds = [*xd_kept, *xd_new]
    grad_gu = weight_grad(xds, [dh_kept, dh_new], 0, width, 0, 2 * ff, groups)
    grad_dn = weight_grad([wa_kept, wa_new], xds, 0, ff, width, width, groups)

    token_grad = home[:, :width].astype(BF16)
    hit = other_routes[:, :, None] == jnp.arange(size, dtype=jnp.int32)[None, None, :]
    gate_home = jnp.sum(jnp.where(hit, home[:, None, width : width + size], 0.0), axis=2)
    return (
        combined[None],
        token_grad[None],
        gate_home.astype(BF16)[None],
        grad_gu[None, None],
        grad_dn[None, None],
    )


def solution(mesh):
    three = P("segment", "expert", None)
    four = P("segment", "expert", None, None)

    return jax.shard_map(
        shards,
        mesh=mesh,
        in_specs=(three,) * 7 + (four,) * 2,
        out_specs=(three,) * 3 + (four,) * 2,
        check_vma=False,
    )
```

```python
import jax
import jax.numpy as jnp
from jax import lax
from jax.experimental import pallas as pl
from jax.experimental.pallas import tpu as pltpu
from jax.sharding import PartitionSpec as P


LANES = 128
F32 = jnp.float32
BF16 = jnp.bfloat16
NT = (((1,), (1,)), ((), ()))
TN = (((0,), (0,)), ((), ()))
VMEM_BYTES = 50 << 20
ANY = pl.BlockSpec(memory_space=pl.ANY)


def after(value, *others):
    return lax.optimization_barrier((value, *others))[0]


def send(array, size, bit):
    return lax.ppermute(array, "expert", [(i, i ^ (1 << bit)) for i in range(size)])


def three_ways(size, count):
    bits = size.bit_length() - 1
    middle = list(range(2, bits - 1))
    small, large = count // 4, 3 * count // 8
    return [
        (0, small, [0, 1, *middle]),
        (small, small + large, [1, *middle, 0]),
        (small + large, count, [*middle, 0, 1]),
    ]


def send_all(arrays, size, parts, step):
    bits = [p[2][step] for p in parts]
    got = [None] * len(arrays)
    for bit in dict.fromkeys(bits):
        which = [i for i, b in enumerate(bits) if b == bit]
        whole = send(jnp.concatenate([arrays[i] for i in which]), size, bit)
        start = 0
        for i in which:
            got[i] = whole[start : start + arrays[i].shape[0]]
            start += arrays[i].shape[0]
    return got


def top_bit(size):
    return size.bit_length() - 2


def spread_rest(kept, size, parts):
    for step in range(len(parts[0][2]) - 1):
        got = send_all(kept, size, parts, step)
        for k in range(len(kept)):
            kept[k] = jnp.concatenate([kept[k], got[k]])
    return kept, send_all(kept, size, parts, -1)


def add(a, b):
    return (a.astype(F32) + b.astype(F32)).astype(BF16)


def merge(kept, got):
    n = kept.shape[0] // 2
    return add(kept[:n], got[:n]), add(kept[n:], got[n:])


def collect_first(kept, away, size, parts, hold):
    got = after(send_all(away, size, parts, -1), *hold)
    return [merge(k, g) for k, g in zip(kept, got)]


def collect_rest(rows, size, parts):
    for step in range(len(parts[0][2]) - 2, -1, -1):
        got = send_all([r[1] for r in rows], size, parts, step)
        rows = [merge(r[0], g) for r, g in zip(rows, got)]
    sections = lax.axis_size("segment")
    cross = lambda flip: [
        (s * size + i, (s ^ 1) * size + (i ^ flip)) for s in range(sections) for i in range(size)
    ]
    own, other = (jnp.concatenate([r[k] for r in rows]) for k in range(2))
    other = lax.ppermute(other, ("segment", "expert"), cross(size // 2))
    own = lax.ppermute(own, ("segment", "expert"), cross(0))
    return own.astype(F32) + other.astype(F32)


def dense_gates(routes, gates, size):
    hit = routes[:, :, None] == jnp.arange(size, dtype=jnp.int32)[None, None, :]
    return jnp.sum(jnp.where(hit, gates[:, :, None].astype(F32), 0.0), axis=1)


def pick(table, at):
    lane = lax.broadcasted_iota(jnp.int32, table.shape, 1)
    return jnp.sum(jnp.where(lane == at, table.astype(F32), 0.0), axis=1, keepdims=True)


def copies_of(pairs, sems, start):
    return [pltpu.make_async_copy(a, b, sems.at[start + i]) for i, (a, b) in enumerate(pairs)]


def begin(made):
    for copy in made:
        copy.start()


def end(made):
    for copy in made:
        copy.wait()


def starts_of(counts):
    return [sum(counts[:i]) for i in range(len(counts))]


def block_start(step, count):
    return step * count if isinstance(step, int) else pl.multiple_of(step * count, 8)


def span(at, count):
    return pl.ds(at if isinstance(at, int) else pl.multiple_of(at, LANES), count)


def row_pairs(pieces, whole, counts, step, at, columns, outward=False):
    pairs = []
    for piece, count, start in zip(pieces, counts, starts_of(counts)):
        outer = piece.at[pl.ds(block_start(step, count), count), span(at, columns)]
        inner = whole.at[pl.ds(start, count)]
        pairs.append((inner, outer) if outward else (outer, inner))
    return pairs


def once(groups, step):
    return pl.when(step == 0) if groups > 1 else lambda run: run()


CHUNKS = 3
PANELS = 4


def weight_copies(wgu_ref, wdn_ref, wgu, wdn, sems, j):
    ff = wdn.shape[0]
    wide = ff // CHUNKS
    pairs = [(wgu_ref.at[:, span(at, wide)], wgu.at[:, span(at, wide)]) for at in (j * wide, ff + j * wide)]
    rows = span(j * wide, wide)
    pairs.append((wdn_ref.at[rows], wdn.at[rows]))
    return copies_of(pairs, sems, 3 * j)


def back_kernel(counts, groups, me_ref, *refs):
    n = len(counts)
    xd_in, tables, (wgu_ref, wdn_ref) = refs[:n], refs[n : 2 * n], refs[2 * n : 2 * n + 2]
    dx_out, (dh_out, wa_out) = refs[2 * n + 2 : 3 * n + 2], refs[3 * n + 2 : 3 * n + 4]
    x, dy, table, wgu, wdn, dx, extra, dh, wa, gate_grad, sems, w_sems, out_sems = refs[3 * n + 4 :]
    me = me_ref[0]
    step = pl.program_id(0) if groups > 1 else 0
    ff, width = wdn.shape
    lanes = table.shape[1]
    rows = x.shape[0]
    weights = lambda j: weight_copies(wgu_ref, wdn_ref, wgu, wdn, w_sems, j)
    first = once(groups, step)
    ins = copies_of(row_pairs(xd_in, x, counts, step, 0, width), sems, 0)
    dys = copies_of(
        row_pairs(xd_in, dy, counts, step, width, width)
        + row_pairs(tables, table, counts, step, width, lanes),
        sems,
        n,
    )
    begin(ins)
    first(lambda: begin(weights(0)))
    begin(dys)

    @first
    def _():
        for j in range(1, CHUNKS):
            begin(weights(j))

    end(ins)
    end(dys)
    wide = ff // CHUNKS
    gate_grad[...] = jnp.zeros_like(gate_grad)

    @pl.loop(0, CHUNKS)
    def _(j):
        first(lambda: end(weights(j)))
        own = span(j * wide, wide)
        also = span(ff + j * wide, wide)
        gate = jnp.dot(x[...], wgu[:, own], preferred_element_type=F32)
        upper = jnp.dot(x[...], wgu[:, also], preferred_element_type=F32)
        back = lax.dot_general(dy[...], wdn[own], NT, preferred_element_type=F32)
        gate_b = pick(table[...], me)
        sigma = jax.nn.sigmoid(gate)
        silu = gate * sigma
        active = silu * upper
        gate_grad[...] += jnp.sum(active * back, axis=1, keepdims=True)
        wa[:, own] = (active * gate_b).astype(BF16)
        d_active = back * gate_b
        dh[:, own] = (d_active * upper * sigma * (1.0 + gate * (1.0 - sigma))).astype(BF16)
        dh[:, also] = (d_active * silu).astype(BF16)

    lane = lax.broadcasted_iota(jnp.int32, (rows, lanes), 1)
    extra[...] = jnp.where(lane == me, gate_grad[...], 0.0).astype(BF16)
    here = pl.ds(block_start(step, rows), rows)
    outs = copies_of(
        row_pairs(dx_out, extra, counts, step, width, lanes, True)
        + [(dh, dh_out.at[here]), (wa, wa_out.at[here])],
        sems,
        3 * n,
    )
    begin(outs)
    panel = width // PANELS

    def panel_copies(p):
        pairs = row_pairs(dx_out, dx.at[p], counts, step, p * panel, panel, True)
        return copies_of(pairs, out_sems, n * p)

    @pl.loop(0, PANELS)
    def _(p):
        dx[p] = lax.dot_general(
            dh[...], wgu[span(p * panel, panel)], NT, preferred_element_type=F32
        ).astype(BF16)
        begin(panel_copies(p))

    end(outs)
    for p in range(PANELS):
        end(panel_copies(p))


def group_counts(pieces, groups):
    return [p.shape[0] // groups for p in pieces]


def back_rows(me, xds, tables, w_gu, w_dn, groups):
    ff, width = w_dn.shape
    lanes = tables[0].shape[1] - width
    counts = group_counts(xds, groups)
    rows = sum(counts)
    n = len(counts)
    total = rows * groups
    shape = jax.ShapeDtypeStruct
    out = pl.pallas_call(
        lambda *refs: back_kernel(counts, groups, *refs),
        grid_spec=pltpu.PrefetchScalarGridSpec(
            num_scalar_prefetch=1,
            grid=(groups,),
            in_specs=[ANY] * (2 * n + 2),
            out_specs=[ANY] * (n + 2),
            scratch_shapes=[
                pltpu.VMEM((rows, width), BF16),
                pltpu.VMEM((rows, width), BF16),
                pltpu.VMEM((rows, lanes), BF16),
                pltpu.VMEM(w_gu.shape, BF16),
                pltpu.VMEM(w_dn.shape, BF16),
                pltpu.VMEM((PANELS, rows, width // PANELS), BF16),
                pltpu.VMEM((rows, lanes), BF16),
                pltpu.VMEM((rows, 2 * ff), BF16),
                pltpu.VMEM((rows, ff), BF16),
                pltpu.VMEM((rows, 1), F32),
                pltpu.SemaphoreType.DMA((4 * n + 2,)),
                pltpu.SemaphoreType.DMA((3 * CHUNKS,)),
                pltpu.SemaphoreType.DMA((n * PANELS,)),
            ],
        ),
        out_shape=[shape((p.shape[0], width + lanes), BF16) for p in xds]
        + [shape((total, 2 * ff), BF16), shape((total, ff), BF16)],
        compiler_params=pltpu.CompilerParams(vmem_limit_bytes=VMEM_BYTES),
        cost_estimate=pl.CostEstimate(
            flops=total * width * ff * 10,
            bytes_accessed=6 * ff * width + total * (6 * width + 4 * lanes + 6 * ff),
            transcendentals=total * ff,
        ),
    )(me, *xds, *tables, w_gu, w_dn)
    return out[:n], out[n], out[n + 1]


def forward_kernel(counts, groups, me_ref, *refs):
    n = len(counts)
    x_in, (wgu_ref, wdn_ref), y_out = refs[:n], refs[n : n + 2], refs[n + 2 : 2 * n + 2]
    x, table, wgu, wdn, act, y, sems, w_sems, out_sems = refs[2 * n + 2 :]
    step = pl.program_id(0) if groups > 1 else 0
    ff, width = wdn.shape
    lanes = table.shape[1]
    weights = lambda j: weight_copies(wgu_ref, wdn_ref, wgu, wdn, w_sems, j)
    first = once(groups, step)
    ins = copies_of(
        row_pairs(x_in, x, counts, step, 0, width)
        + row_pairs(x_in, table, counts, step, width, lanes),
        sems,
        0,
    )
    begin(ins)

    @first
    def _():
        for j in range(CHUNKS):
            begin(weights(j))

    end(ins)
    wide = ff // CHUNKS

    @pl.loop(0, CHUNKS)
    def _(j):
        first(lambda: end(weights(j)))
        own = span(j * wide, wide)
        also = span(ff + j * wide, wide)
        gate = jnp.dot(x[...], wgu[:, own], preferred_element_type=F32)
        upper = jnp.dot(x[...], wgu[:, also], preferred_element_type=F32)
        act[:, own] = (gate * jax.nn.sigmoid(gate) * upper).astype(BF16)

    panel = width // PANELS

    def panel_copies(p):
        pairs = row_pairs(y_out, y.at[p], counts, step, p * panel, panel, True)
        return copies_of(pairs, out_sems, n * p)

    @pl.loop(0, PANELS)
    def _(p):
        gate_f = pick(table[...], me_ref[1])
        cols = span(p * panel, panel)
        y[p] = (jnp.dot(act[...], wdn[:, cols], preferred_element_type=F32) * gate_f).astype(BF16)
        begin(panel_copies(p))

    for p in range(PANELS):
        end(panel_copies(p))


def forward_rows(me, xs, w_gu, w_dn, groups):
    ff, width = w_dn.shape
    lanes = xs[0].shape[1] - width
    counts = group_counts(xs, groups)
    rows = sum(counts)
    n = len(counts)
    total = rows * groups
    return pl.pallas_call(
        lambda *refs: forward_kernel(counts, groups, *refs),
        grid_spec=pltpu.PrefetchScalarGridSpec(
            num_scalar_prefetch=1,
            grid=(groups,),
            in_specs=[ANY] * (n + 2),
            out_specs=[ANY] * n,
            scratch_shapes=[
                pltpu.VMEM((rows, width), BF16),
                pltpu.VMEM((rows, lanes), BF16),
                pltpu.VMEM(w_gu.shape, BF16),
                pltpu.VMEM(w_dn.shape, BF16),
                pltpu.VMEM((rows, ff), BF16),
                pltpu.VMEM((PANELS, rows, width // PANELS), BF16),
                pltpu.SemaphoreType.DMA((2 * n,)),
                pltpu.SemaphoreType.DMA((3 * CHUNKS,)),
                pltpu.SemaphoreType.DMA((n * PANELS,)),
            ],
        ),
        out_shape=[jax.ShapeDtypeStruct((p.shape[0], width), BF16) for p in xs],
        compiler_params=pltpu.CompilerParams(vmem_limit_bytes=VMEM_BYTES),
        cost_estimate=pl.CostEstimate(
            flops=total * width * ff * 6,
            bytes_accessed=6 * ff * width + total * 4 * width,
            transcendentals=total * ff,
        ),
    )(me, *xs, w_gu, w_dn)


def weight_kernel(lefts, rights, left_at, right_at, groups, *refs):
    n, m = len(lefts), len(rights)
    left_in, right_in, out_ref = refs[:n], refs[n : n + m], refs[n + m]
    left, right, stage = refs[n + m + 1 : n + m + 4]
    sems, left_sems, out_sems = refs[-3:]
    step = pl.program_id(0) if groups > 1 else 0
    tiles, _, tile = left.shape
    rights_made = copies_of(row_pairs(right_in, right, rights, step, right_at, right.shape[1]), sems, 0)
    begin(rights_made)

    def left_copies(t):
        pairs = row_pairs(left_in, left.at[t], lefts, step, left_at + t * tile, tile)
        return copies_of(pairs, left_sems, n * t)

    def out_copy(t):
        return copies_of([(stage.at[t], out_ref.at[span(t * tile, tile)])], out_sems, t)

    for t in range(tiles):
        begin(left_copies(t))
    end(rights_made)

    @pl.loop(0, tiles)
    def _(t):
        end(left_copies(t))
        part = lax.dot_general(left[t], right[...], TN, preferred_element_type=F32)
        if groups > 1:
            total = refs[n + m + 4]
            part += jnp.where(step == 0, 0.0, total[t])
            total[t] = part
            stage[t] = part.astype(BF16)
            pl.when(step == groups - 1)(lambda: begin(out_copy(t)))
        else:
            stage[t] = part.astype(BF16)
            begin(out_copy(t))

    def finish():
        for t in range(tiles):
            end(out_copy(t))

    pl.when(step == groups - 1)(finish) if groups > 1 else finish()


def weight_grad(lefts, rights, left_at, left_wide, right_at, right_wide, groups):
    left_counts = group_counts(lefts, groups)
    right_counts = group_counts(rights, groups)
    rows = sum(left_counts)
    tile = 256
    tiles = left_wide // tile
    scratch = [
        pltpu.VMEM((tiles, rows, tile), BF16),
        pltpu.VMEM((rows, right_wide), BF16),
        pltpu.VMEM((tiles, tile, right_wide), BF16),
    ]
    if groups > 1:
        scratch.append(pltpu.VMEM((tiles, tile, right_wide), F32))
    scratch += [pltpu.SemaphoreType.DMA((k,)) for k in (len(rights), tiles * len(lefts), tiles)]
    return pl.pallas_call(
        lambda *refs: weight_kernel(left_counts, right_counts, left_at, right_at, groups, *refs),
        grid=(groups,),
        in_specs=[ANY] * (len(lefts) + len(rights)),
        out_specs=ANY,
        out_shape=jax.ShapeDtypeStruct((left_wide, right_wide), BF16),
        scratch_shapes=scratch,
        compiler_params=pltpu.CompilerParams(vmem_limit_bytes=VMEM_BYTES),
        cost_estimate=pl.CostEstimate(
            flops=2 * rows * groups * left_wide * right_wide,
            bytes_accessed=2 * rows * groups * (left_wide + right_wide) + 2 * left_wide * right_wide,
            transcendentals=0,
        ),
    )(*lefts, *rights)


def shards(
    fwd_tokens,
    fwd_routes,
    fwd_gates,
    bwd_tokens,
    bwd_routes,
    bwd_gates,
    cotangent,
    w_gate_up,
    w_down,
):
    size = lax.axis_size("expert")
    me = lax.axis_index("expert")
    count, width = fwd_tokens.shape[1:]
    w_gu = w_gate_up[0, 0]
    w_dn = w_down[0, 0]
    ff = w_dn.shape[0]
    groups = max(1, size // 16)
    sections = lax.axis_size("segment")
    swap = [(s, s ^ 1) for s in range(sections)]
    table = jnp.concatenate(
        [
            dense_gates(bwd_routes[0], bwd_gates[0], size),
            dense_gates(fwd_routes[0], fwd_gates[0], size),
        ],
        axis=1,
    )
    table = jnp.pad(table, ((0, 0), (0, -table.shape[1] % LANES))).astype(BF16)
    places = jnp.stack([me, me + size]).astype(jnp.int32)
    parts = three_ways(size, count)
    first = send(fwd_tokens[0], size, top_bit(size))
    tables = table, send(table, size, top_bit(size))
    pair = [jnp.concatenate(both, axis=1) for both in zip((fwd_tokens[0], first), tables)]
    pair = [jnp.concatenate([p[a:b] for p in pair]) for a, b, _ in parts]
    xf_kept, xf_new = spread_rest(pair, size, parts)
    y_kept = forward_rows(places, xf_kept, w_gu, w_dn, groups)

    def forward_new(xf_new):
        return forward_rows(places, xf_new, w_gu, w_dn, groups)

    def forward_first(y_kept, y_new, *hold):
        return collect_first(y_kept, y_new, size, parts, hold)

    def forward_last(rows):
        return collect_rest(rows, size, parts).astype(BF16)

    xd_in = jnp.concatenate([bwd_tokens[0], cotangent[0]], axis=1)
    if groups > 1:
        y_new = forward_new(after(xf_new, y_kept))
        combined = forward_last(forward_first(y_kept, y_new))
        xd_in = after(xd_in, combined)
    xd_in = after(xd_in, first)
    pair = xd_in, send(xd_in, size, top_bit(size))
    pair = [jnp.concatenate([p[a:b] for p in pair]) for a, b, _ in parts]
    xd_kept, xd_new = spread_rest(pair, size, parts)
    other_routes = lax.ppermute(bwd_routes[0], "segment", swap)

    if groups == 1:
        y_new = forward_new(after(xf_new, y_kept))
        xd_kept = after(xd_kept, y_new)
    dx_kept, dh_kept, wa_kept = back_rows(places, xd_kept, xf_kept, w_gu, w_dn, groups)
    xd_new = after(xd_new, dx_kept)
    if groups == 1:
        y_new = [y_new[0], *after(y_new[1:], xd_new)]
    dx_new, dh_new, wa_new = back_rows(places, xd_new, xf_new, w_gu, w_dn, groups)
    if groups == 1:
        comb_rows = forward_first(y_kept, y_new, dx_new)
        wa_kept = after(wa_kept, comb_rows)
    home_rows = collect_first(dx_kept, dx_new, size, parts, ())
    if groups == 1:
        combined = forward_last(comb_rows)
    home = collect_rest(home_rows, size, parts)

    xds = [*xd_kept, *xd_new]
    grad_gu = weight_grad(xds, [dh_kept, dh_new], 0, width, 0, 2 * ff, groups)
    grad_dn = weight_grad([wa_kept, wa_new], xds, 0, ff, width, width, groups)

    token_grad = home[:, :width].astype(BF16)
    hit = other_routes[:, :, None] == jnp.arange(size, dtype=jnp.int32)[None, None, :]
    gate_home = jnp.sum(jnp.where(hit, home[:, None, width : width + size], 0.0), axis=2)
    return (
        combined[None],
        token_grad[None],
        gate_home.astype(BF16)[None],
        grad_gu[None, None],
        grad_dn[None, None],
    )


def solution(mesh):
    three = P("segment", "expert", None)
    four = P("segment", "expert", None, None)

    return jax.shard_map(
        shards,
        mesh=mesh,
        in_specs=(three,) * 7 + (four,) * 2,
        out_specs=(three,) * 3 + (four,) * 2,
        check_vma=False,
    )
```
